32 devices in a mesh: rve: 4 (over y, x), slab: 8 (over z, core).
Axes of the slice: x: 2, y: 2, z: 4, core: 2. Of those that a mesh axis runs over, the one named last changes fastest.
Arguments:
- plastic_strain: float32 [6, 4, 96, 9216], P(None, 'rve', 'slab'), may hold values from -2 to 2
- hardening_var: float32 [4, 96, 9216], P('rve', 'slab'), may hold values from 0 to 1
- strain_start: float32 [6, 4, 96, 9216], P(None, 'rve', 'slab'), may hold values from -6 to 6
- strain_step: float32 [6, 4, 96, 9216], P(None, 'rve', 'slab'), may hold values from -4 to 4
- shear_mod: float32 [4, 96, 9216], P('rve', 'slab'), may hold values from 0.5 to 2
- bulk_mod: float32 [4, 96, 9216], P('rve', 'slab'), may hold values from 1 to 4
- yield_stress: float32 [4, 96, 9216], P('rve', 'slab'), may hold values from 0.5 to 4
- substeps: int32 [4, 384], replicated, may hold values from 1 to 8, as said below
- pull_group: int32 [4, 16], replicated, may hold values from 0 to 3, as said below
- pull_block: int32 [4, 16], replicated, may hold values from 0 to 383, as said below
- owner: int32 [4], replicated, may hold values from 0 to 3
Outputs:
- correction: float32 [3, 4, 96, 9216], P(None, 'rve', 'slab')
- inbox: float32 [7, 4, 16, 2304], P(None, 'rve', 'slab')
- element_sums: float32 [4, 42], P('rve')
The draws below stay inside these ranges and needn't reach their ends.
Inputs may be any that keep to these rules, and one draw needn't show every extreme that they name: `substeps`: every RVE has a block with exactly its largest count, and some RVE reaches 8. `pull_group`: for each group g and each slab s, the 2 slots k with k // 2 = s name distinct source groups. `pull_block`: slot k names a block of z-slab k // 2: an id from (k // 2) * 4 * 12 to (k // 2 + 1) * 4 * 12 - 1.
All inputs are finite; a program needn't handle non-finite values.
Results may differ from the reference program's by a relative error of at most 0.0003.
Values sent between devices are 32-bit elements; how exact they have to be, the bound alone decides.
A program may use at most 192 MiB of HBM per device.

```python
import math
import jax
import jax.numpy as jnp
from jax import lax

NVX = 96
NZ = 96
ITERS = 5
SUBMAX = 8
SZ = 12
PLANE = 9216
BLK = 2304
NBLK = 384
RVES = 4
IN_DEV = 2
INBOX = 16


def pull_plan(key):
    slab_total = INBOX // IN_DEV
    key_list = jax.random.split(jax.random.fold_in(key, 11), RVES * slab_total)

    def choose(single):
        return jax.random.permutation(single, RVES)[:IN_DEV]
    sources = jax.vmap(choose)(key_list).reshape(RVES, INBOX)
    offsets = jax.random.randint(jax.random.fold_in(key, 12), (RVES, INBOX), 0, 4 * SZ)
    slots = jnp.arange(INBOX)
    blocks = (slots // IN_DEV)[None, :] * (4 * SZ) + offsets
    return (sources.astype(jnp.int32), blocks.astype(jnp.int32))


def draw_pull_group(key, part):
    return pull_plan(key)[0]


def draw_pull_block(key, part):
    return pull_plan(key)[1]


def draw_substeps(key, part):
    level = jax.random.randint(jax.random.fold_in(key, 21), (RVES,), 1, SUBMAX + 1)
    forced = jax.random.randint(jax.random.fold_in(key, 22), (), 0, RVES)
    level = jnp.where(jnp.arange(RVES) == forced, SUBMAX, level)
    raw = jax.random.randint(jax.random.fold_in(key, 23), (RVES, NBLK), 0, 1000000) % level[:, None] + 1
    special = jax.random.randint(jax.random.fold_in(key, 24), (RVES,), 0, NBLK)
    costs = jnp.where(jnp.arange(NBLK)[None, :] == special[:, None], level[:, None], raw)
    return costs.astype(jnp.int32)


def with_ends(values, rng, low, largest):
    extent = values.shape
    index_at = [jax.random.randint(jax.random.fold_in(rng, axis), (), 0, extent[axis]) for axis in range(len(extent))]
    values = values.at[tuple(index_at)].set(low)
    longest = extent.index(max(extent))
    index_at[longest] = (index_at[longest] + 1) % extent[longest]
    return values.at[tuple(index_at)].set(largest)


def block_levels(stream_key, extent, cuts, low, high):
    loudness = 1.0
    for position, shards_of in cuts:
        draws = jax.random.uniform(jax.random.fold_in(jax.random.fold_in(stream_key, 6), position), (shards_of,), jnp.float32, low / len(cuts), high / len(cuts))
        loudness = loudness * jnp.repeat(jnp.exp(draws), extent[position] // shards_of).reshape((-1,) + (1,) * (len(extent) - 1 - position))
    return loudness


def bell_draw(key, shape, deviation, most, shards=(), kind=jnp.bfloat16):
    result = deviation * jax.random.normal(key, shape, jnp.float32)
    if shards:
        result = result * block_levels(key, shape, shards, -0.22, 0.18)
    return jnp.clip(result, -most, most).astype(kind)


def setup_inputs(seed: int = 0) -> dict:
    splits = jax.random.split(jax.random.key(seed), 12)
    plastic_strain = bell_draw(splits[0], (6, RVES, NZ, PLANE), 0.3, 2.0, ((1, 4), (2, 8)), jnp.float32)
    hardening_var = jnp.clip(1.0 * jax.random.uniform(splits[1], (RVES, NZ, PLANE), jnp.float32) ** block_levels(splits[1], (RVES, NZ, PLANE), ((0, 4), (1, 8)), -0.2, 0.2), 0.0, 1.0)
    strain_start = bell_draw(splits[2], (6, RVES, NZ, PLANE), 1.0, 6.0, ((1, 4), (2, 8)), jnp.float32)
    strain_step = bell_draw(splits[3], (6, RVES, NZ, PLANE), 0.5, 4.0, ((1, 4), (2, 8)), jnp.float32)
    shear_mod = jnp.clip(jnp.exp(math.log(2.0) - 1.3862944 * jax.random.uniform(splits[4], (RVES, NZ, PLANE), jnp.float32) ** block_levels(splits[4], (RVES, NZ, PLANE), ((0, 4), (1, 8)), -0.2, 0.2)), 0.5, 2.0)
    bulk_mod = jnp.clip(jnp.exp(math.log(4.0) - 1.3862944 * jax.random.uniform(splits[5], (RVES, NZ, PLANE), jnp.float32) ** block_levels(splits[5], (RVES, NZ, PLANE), ((0, 4), (1, 8)), -0.2, 0.2)), 1.0, 4.0)
    yield_stress = jnp.clip(jnp.exp(math.log(4.0) - 2.0794415 * jax.random.uniform(splits[6], (RVES, NZ, PLANE), jnp.float32) ** block_levels(splits[6], (RVES, NZ, PLANE), ((0, 4), (1, 8)), -0.2, 0.2)), 0.5, 4.0)
    substeps = draw_substeps(jax.random.fold_in(splits[11], 71), 0)
    pull_group = draw_pull_group(jax.random.fold_in(splits[11], 71), 0)
    pull_block = draw_pull_block(jax.random.fold_in(splits[11], 71), 0)
    owner = with_ends(jax.random.randint(splits[10], (RVES,), 0, RVES), jax.random.fold_in(splits[10], 1), 0, RVES - 1).astype(jnp.int32)
    return {"plastic_strain": plastic_strain, "hardening_var": hardening_var, "strain_start": strain_start, "strain_step": strain_step, "shear_mod": shear_mod, "bulk_mod": bulk_mod, "yield_stress": yield_stress, "substeps": substeps, "pull_group": pull_group, "pull_block": pull_block, "owner": owner}


hard_ratio = 0.3
mass_weight = 0.05
root_two_thirds = math.sqrt(2.0 / 3.0)
half_root = 1.0 / math.sqrt(2.0)

def stencil_offsets():
    listing = []
    for depth_step in (-1, 0, 1):
        for row_step in (-1, 0, 1):
            for column_step in (-1, 0, 1):
                reach = abs(depth_step) + abs(row_step) + abs(column_step)
                if reach > 0:
                    listing.append((depth_step, row_step, column_step, (1.0, 0.5, 0.25)[reach - 1]))
    return listing

def plane_shift(values, row_step, column_step):
    if row_step != 0:
        values = jnp.roll(values, -row_step * NVX, axis=-1)
    if column_step != 0:
        column = jnp.arange(PLANE) % NVX
        plain = jnp.roll(values, -column_step, axis=-1)
        wrapped = jnp.roll(values, column_step * NVX - column_step, axis=-1)
        border = NVX - 1 if column_step > 0 else 0
        values = jnp.where(column == border, wrapped, plain)
    return values

def trace_vector(ndim):
    return jnp.array([1.0, 1.0, 1.0, 0.0, 0.0, 0.0], jnp.float32).reshape((6,) + (1,) * (ndim - 1))

def deviator_of(strain, plastic):
    elastic = strain - plastic
    volume = elastic[0] + elastic[1] + elastic[2]
    return (elastic - volume / 3.0 * trace_vector(strain.ndim), volume)

def return_map(plastic, hardening, strain_begin, strain_delta, shear_field, bulk_field, yield_field, count, turns):
    harden = hard_ratio * shear_field

    def substep(turn, carry):
        plastic_now, hardening_now, increment, direction, floored = carry
        turn_float = jnp.asarray(turn).astype(jnp.float32)
        strain = strain_begin + (turn_float + 1.0) / count * strain_delta
        deviator, volume = deviator_of(strain, plastic_now)
        trial = 2.0 * shear_field * deviator
        magnitude = jnp.sqrt(lax.optimization_barrier(jnp.sum(trial * trial, axis=0)))
        excess = magnitude - root_two_thirds * (yield_field + harden * hardening_now)
        active = turn_float < count
        new_increment = jnp.maximum(excess, 0.0) / (2.0 * shear_field + 2.0 / 3.0 * harden)
        new_floored = jnp.maximum(magnitude, root_two_thirds * yield_field)
        new_direction = trial / new_floored
        new_increment = jnp.where(active, new_increment, 0.0)
        plastic_now = plastic_now + new_increment * new_direction
        hardening_now = hardening_now + root_two_thirds * new_increment
        increment = jnp.where(active, new_increment, increment)
        direction = jnp.where(active, new_direction, direction)
        floored = jnp.where(active, new_floored, floored)
        return (plastic_now, hardening_now, increment, direction, floored)
    start = (plastic, hardening, jnp.zeros_like(hardening), jnp.zeros_like(plastic), jnp.ones_like(hardening))
    plastic_new, hardening_new, increment, direction, floored = lax.fori_loop(0, turns, substep, start)
    deviator, volume = deviator_of(strain_begin + strain_delta, plastic_new)
    stress = bulk_field * volume * trace_vector(plastic.ndim) + 2.0 * shear_field * deviator
    theta = 1.0 - 2.0 * shear_field * increment / floored
    coefficient = shear_field * theta
    weight = shear_field * (theta - 1.0)
    return (stress, coefficient, plastic_new, hardening_new, weight, direction)

def rhs_from(stress, depth_diff):
    row_diff = 0.5 * (plane_shift(stress, 1, 0) - plane_shift(stress, -1, 0))
    column_diff = 0.5 * (plane_shift(stress, 0, 1) - plane_shift(stress, 0, -1))
    return jnp.stack([column_diff[0] + half_root * (row_diff[5] + depth_diff[4]), half_root * (column_diff[5] + depth_diff[3]) + row_diff[1], half_root * (column_diff[4] + row_diff[3]) + depth_diff[2]])

def apply_operator(field, coefficient):
    total = mass_weight * coefficient * field
    for depth_step, row_step, column_step, weight in stencil_offsets():
        other = plane_shift(jnp.roll(field, -depth_step, axis=-2), row_step, column_step)
        other_coef = plane_shift(jnp.roll(coefficient, -depth_step, axis=-2), row_step, column_step)
        total = total + 0.5 * weight * (coefficient + other_coef) * (field - other)
    return total

def finish(sums):
    trace_vec = jnp.array([1.0, 1.0, 1.0, 0.0, 0.0, 0.0], jnp.float32)
    outer = trace_vec[:, None] * trace_vec[None, :]
    projector = jnp.eye(6, dtype=jnp.float32) - outer / 3.0
    tangent = sums[6] * outer + 2.0 * sums[7] * projector + 2.0 * sums[8:].reshape(6, 6)
    return jnp.concatenate([sums[:6], tangent.reshape(36)])

def one_rve(items):
    plastic, hardening, begin, delta, shear_field, bulk_field, yield_field, costs = items
    count = jnp.broadcast_to(costs.astype(jnp.float32)[:, None], (NBLK, BLK)).reshape(NZ, PLANE)
    stress, coefficient, plastic_new, hardening_new, weight, direction = return_map(plastic, hardening, begin, delta, shear_field, bulk_field, yield_field, count, SUBMAX)
    volume = float(NZ * PLANE)
    flat_direction = direction.reshape(6, NZ * PLANE)
    coupling = jnp.dot(weight.reshape(1, NZ * PLANE) * flat_direction, flat_direction.T, precision=lax.Precision.HIGHEST)
    sums = jnp.concatenate([lax.optimization_barrier(jnp.sum(stress, axis=(1, 2))), jnp.sum(bulk_field)[None], jnp.sum(coefficient)[None], coupling.reshape(36)]) / volume
    depth_diff = 0.5 * (jnp.roll(stress, -1, axis=-2) - jnp.roll(stress, 1, axis=-2))
    rhs = rhs_from(stress, depth_diff)
    solution = jnp.zeros_like(rhs)
    residual = rhs
    direction_cg = rhs
    norm_now = jnp.sum(residual * residual)
    for turn in range(ITERS):
        image = apply_operator(direction_cg, coefficient)
        alpha = norm_now / jnp.sum(direction_cg * image)
        solution = solution + alpha * direction_cg
        residual = residual - alpha * image
        norm_next = jnp.sum(residual * residual)
        direction_cg = residual + norm_next / norm_now * direction_cg
        norm_now = norm_next
    history = jnp.concatenate([plastic_new, hardening_new[None]], axis=0)
    return (solution, history, finish(sums))

def reference(plastic_strain, hardening_var, strain_start, strain_step, shear_mod, bulk_mod, yield_stress, substeps, pull_group, pull_block, owner):
    items = (jnp.moveaxis(plastic_strain, 1, 0), hardening_var, jnp.moveaxis(strain_start, 1, 0), jnp.moveaxis(strain_step, 1, 0), shear_mod, bulk_mod, yield_stress, substeps)
    solutions, histories, summaries = lax.map(one_rve, items)
    correction = jnp.moveaxis(solutions, 0, 1)
    blocks = histories.reshape(RVES, 7, NBLK, BLK)
    picked = blocks[pull_group, :, pull_block, :]
    inbox = jnp.transpose(picked, (2, 0, 1, 3))
    table = (owner[None, :] == jnp.arange(RVES)[:, None]).astype(jnp.float32)
    element_sums = jnp.dot(table, summaries, precision=lax.Precision.HIGHEST)
    return (correction, inbox, element_sums)
```

```python
import functools
import math

import jax
import jax.numpy as jnp
from jax import lax
from jax.experimental import pallas as pl
from jax.experimental.pallas import tpu as pltpu
from jax.sharding import PartitionSpec as P

NVX = 96
ITERS = 5
PLANE = 9216
BLK = 2304
LANES = 128
PART = 24
MEAN_LANE = 42
SHIFT = 12.0
MESH = pl.DeviceIdType.MESH

hard_ratio = 0.3
mass_weight = 0.05
root_two_thirds = math.sqrt(2.0 / 3.0)
half_root = 1.0 / math.sqrt(2.0)
KEPT = (0, 1, 3, 4, 5)
PAIRS = tuple((i, j) for i in range(5) for j in range(i, 5))


def lane_id(rows):
    return lax.broadcasted_iota(jnp.int32, (rows, LANES), 1)


def unpack_rows(a, b, c):
    lane = lane_id(a.shape[0])
    plain = (
        a,
        pltpu.roll(jnp.where(lane >= 96, a, b), 32, 1),
        pltpu.roll(jnp.where(lane >= 64, b, c), 64, 1),
        pltpu.roll(c, 96, 1),
    )
    out = []
    for row in plain:
        halo = jnp.where(lane < 112, pltpu.roll(row, 96, 1), pltpu.roll(row, 32, 1))
        out.append(jnp.where(lane < 96, row, halo))
    return out


def pack_rows(rows4):
    t0, t1, t2, t3 = rows4
    lane = lane_id(t0.shape[0])
    r1, r2, r3 = pltpu.roll(t1, 96, 1), pltpu.roll(t2, 64, 1), pltpu.roll(t3, 32, 1)
    return (
        jnp.where(lane < 96, t0, r1),
        jnp.where(lane < 64, r1, r2),
        jnp.where(lane < 32, r2, r3),
    )


def material_kernel(
    depth, volume, in_dev, planes,
    sub_ref, pg_ref, pb_ref, p_ref, h_ref, b_ref, d_ref, g_ref, k_ref, y_ref,
    st_ref, pick_ref, sum_ref,
    acc_ref, hist_ref, wait_ref, dev_ref, del_ref, lev_ref, lev0_ref, tmp_ref,
):
    step = pl.program_id(0)
    group = lax.axis_index("rve")
    slab = lax.axis_index("slab")
    groups = pg_ref.shape[0]
    blocks_dev = 4 * depth
    tiles = PLANE // LANES
    parts = tuple(slice(t, t + PART) for t in range(0, tiles, PART))
    quarter_rows = BLK // LANES

    @pl.when(step == 0)
    def _():
        acc_ref[...] = jnp.zeros_like(acc_ref)

    def dev_parts(ref, z, rows, other=None):
        vals = []
        for c in range(6):
            v = ref[c, z, rows]
            if other is not None:
                v = v - other[c, z, rows]
            vals.append(v)
        trace = vals[0] + vals[1] + vals[2]
        third = trace * (1.0 / 3.0)
        return [vals[c] - third if c < 3 else vals[c] for c in range(6)], trace

    def trial(rows):
        dd = [dev_ref[i, rows] + del_ref[i, rows] for i in range(5)]
        square = (
            2.0 * (dd[0] * (dd[0] + dd[1]) + dd[1] * dd[1])
            + dd[2] * dd[2] + dd[3] * dd[3] + dd[4] * dd[4]
        )
        square = jnp.maximum(square, 1e-30)
        return dd, square, lax.rsqrt(square)

    def one_plane(z, _):
        base = slab * blocks_dev + (step * planes + z) * 4
        counts = [sub_ref[group, base + q] for q in range(4)]
        turns = jnp.maximum(
            jnp.maximum(counts[0], counts[1]), jnp.maximum(counts[2], counts[3])
        )
        for rows in parts:
            row = lax.broadcasted_iota(jnp.int32, (PART, LANES), 0) + rows.start
            count = jnp.full((PART, LANES), counts[0], jnp.int32)
            for q in range(1, 4):
                count = jnp.where(row >= q * quarter_rows, counts[q], count)
            inv = 1.0 / count.astype(jnp.float32)
            waiting = turns - count
            wait_ref[rows] = waiting
            waiting_f = waiting.astype(jnp.float32)
            dev0, _ = dev_parts(b_ref, z, rows, p_ref)
            devs, _ = dev_parts(d_ref, z, rows)
            for i, c in enumerate(KEPT):
                delta = devs[c] * inv
                del_ref[i, rows] = delta
                dev_ref[i, rows] = dev0[c] - waiting_f * delta
            level0 = (11.0 * root_two_thirds / 2.2) * (
                y_ref[z, rows] / g_ref[z, rows] + hard_ratio * h_ref[z, rows]
            )
            lev_ref[rows] = level0
            lev0_ref[rows] = level0

        def substep(turn, _):
            for rows in parts:
                dd, square, rs = trial(rows)
                level = lev_ref[rows]
                fac = jnp.minimum((1.0 + level * rs) * (1.0 / 11.0), 1.0)
                fac = jnp.where(turn >= wait_ref[rows], fac, 1.0)
                lev_ref[rows] = level + (1.0 - fac) * (square * rs)
                for i in range(5):
                    dev_ref[i, rows] = fac * dd[i]
            return 0

        lax.fori_loop(0, turns - 1, substep, 0)
        sums = [None] * (8 + len(PAIRS))
        for rows in parts:
            dd, square, rs = trial(rows)
            level = lev_ref[rows]
            fac = jnp.minimum((1.0 + level * rs) * (1.0 / 11.0), 1.0)
            level = level + (1.0 - fac) * (square * rs)
            fin = [fac * v for v in dd]
            mu = g_ref[z, rows]
            coef = mu * fac
            weight = (coef - mu) * (rs * rs)
            bulk = k_ref[z, rows]
            dev0, tr0 = dev_parts(b_ref, z, rows, p_ref)
            devs, trs = dev_parts(d_ref, z, rows)
            vol = bulk * (tr0 + trs)
            two_mu = 2.0 * mu
            ms = [two_mu * v for v in fin]
            wn = [weight * v for v in dd]
            ms6 = [ms[0], ms[1], -(ms[0] + ms[1]), ms[2], ms[3], ms[4]]
            fin6 = [fin[0], fin[1], -(fin[0] + fin[1]), fin[2], fin[3], fin[4]]
            for c in range(6):
                tmp_ref[c, rows] = ms6[c] + vol if c < 3 else ms6[c]
                hist_ref[c, z, rows] = p_ref[c, z, rows] + (dev0[c] + devs[c] - fin6[c])
            tmp_ref[6, rows] = coef
            hist_ref[6, z, rows] = h_ref[z, rows] + root_two_thirds * (level - lev0_ref[rows])
            terms = [vol, bulk, coef] + ms + [wn[i] * dd[j] for i, j in PAIRS]
            for t, v in enumerate(terms):
                for o in range(0, PART, 8):
                    piece = v[o : o + 8]
                    sums[t] = piece if sums[t] is None else sums[t] + piece
        for t, v in enumerate(sums):
            acc_ref[t] += v

        for f in range(7):
            for g in range(tiles // 24):
                a, b, c = (tmp_ref[f, pl.ds(3 * g + k, 8, stride=9)] for k in range(3))
                for r, rowv in enumerate(unpack_rows(a, b, c)):
                    at = 8 * (4 * g + r)
                    st_ref[f, z, at : at + 8] = rowv
        return 0

    lax.fori_loop(0, planes, one_plane, 0)

    for g in range(groups):
        chosen = jnp.int32(0)
        for j in range(in_dev):
            slot = slab * in_dev + j
            chosen = jnp.where(
                pg_ref[g, slot] == group, pb_ref[g, slot] - slab * blocks_dev, chosen
            )
        z = chosen // 4 - step * planes

        @pl.when((z >= 0) & (z < planes))
        def _():
            for q in range(4):

                @pl.when(chosen % 4 == q)
                def _():
                    for c in range(7):
                        pick_ref[g, c] = hist_ref[c, z, q * quarter_rows : (q + 1) * quarter_rows]

    @pl.when(step == pl.num_programs(0) - 1)
    def _():
        tot = [
            jnp.sum(acc_ref[t], axis=(0, 1), keepdims=True) * (1.0 / volume)
            for t in range(8 + len(PAIRS))
        ]
        vol, bulk, coef = tot[0], tot[1], tot[2]
        ms = tot[3:8]
        stress = [vol + ms[0], vol + ms[1], vol - ms[0] - ms[1], ms[2], ms[3], ms[4]]
        table = {}
        for t, (i, j) in enumerate(PAIRS):
            table[(KEPT[i], KEPT[j])] = tot[8 + t]
            table[(KEPT[j], KEPT[i])] = tot[8 + t]
        for j in KEPT:
            table[(2, j)] = -(table[(0, j)] + table[(1, j)])
            table[(j, 2)] = table[(2, j)]
        table[(2, 2)] = -(table[(2, 0)] + table[(2, 1)])
        lane = lane_id(1)
        row = jnp.zeros((1, LANES), jnp.float32)
        for c in range(6):
            row = jnp.where(lane == c, stress[c], row)
        for i in range(6):
            for j in range(6):
                v = 2.0 * table[(i, j)]
                if i == j:
                    v = v + 2.0 * coef
                if i < 3 and j < 3:
                    v = v + bulk - (2.0 / 3.0) * coef
                row = jnp.where(lane == 6 + 6 * i + j, v, row)
        sum_ref[...] = jnp.where(lane == MEAN_LANE, coef, row)


def ring_next(pieces):
    return pieces[1:] + [pltpu.roll(pieces[0], 7, 0)]


def ring_prev(pieces):
    return [pltpu.roll(pieces[-1], 1, 0)] + pieces[:-1]


def cut(v):
    return [v[i : i + 8] for i in range(0, NVX, 8)]


def spread(pieces):
    p = [x + y for x, y in zip(pieces, ring_next(pieces))]
    p = [x + y for x, y in zip(p, ring_prev(p))]
    q = [x + pltpu.roll(x, LANES - 1, 1) for x in p]
    return [x + pltpu.roll(x, 1, 1) for x in q]


def inner(a, b):
    total = a[0] * b[0]
    for x, y in zip(a[1:], b[1:]):
        total = total + x * y
    return total


def combine(moments, shift):
    one = jnp.ones_like(moments[0])
    res_c, dir_c, out = [one], [one], []
    res_m, dir_m = list(moments), list(moments)
    norm = moments[0]
    for turn in range(ITERS):
        image_m = [shift * x + y for x, y in zip(dir_m, dir_m[1:])]
        alpha = norm / inner(dir_c, image_m)
        grown = out + [jnp.zeros_like(one)]
        out = [x + alpha * y for x, y in zip(grown, dir_c)]
        if turn == ITERS - 1:
            return out
        image_c = [shift * dir_c[0]]
        image_c += [shift * x + y for x, y in zip(dir_c[1:], dir_c)] + [dir_c[-1]]
        res_c = [x - alpha * y for x, y in zip(res_c, image_c)] + [-alpha * image_c[-1]]
        res_m = [x - alpha * y for x, y in zip(res_m, image_m)]
        norm_next = inner(res_c, res_m)
        beta = norm_next / norm
        norm = norm_next
        dir_c = [x + beta * y for x, y in zip(res_c, dir_c)] + [res_c[-1]]
        dir_m = [x + beta * y for x, y in zip(res_m, dir_m)]


def solve_kernel(
    depth, groups, slabs, in_dev,
    pg_ref, own_ref, st_ref, pick_ref, sum_ref,
    out_ref, inbox_ref, elem_ref,
    sh, c8, ee, vv, ps, red, ms, mr, ab, es, eo,
    nsend, nrecv, rsend, rrecv, bsend, brecv, esend, erecv,
):
    group = lax.axis_index("rve")
    slab = lax.axis_index("slab")
    up = lax.rem(slab + 1, slabs)
    down = lax.rem(slab + slabs - 1, slabs)
    last = depth - 1

    barrier = pltpu.get_barrier_semaphore()
    for k in range(1, slabs):
        pl.semaphore_signal(
            barrier, inc=1, device_id={"slab": lax.rem(slab + k, slabs)}, device_id_type=MESH
        )
    for k in range(1, groups):
        pl.semaphore_signal(
            barrier, inc=1, device_id={"rve": lax.rem(group + k, groups)}, device_id_type=MESH
        )
    pl.semaphore_wait(barrier, slabs + groups - 2)

    def remote(src, dst, ssem, rsem, axis, to):
        return pltpu.make_async_remote_copy(
            src_ref=src, dst_ref=dst, send_sem=ssem, recv_sem=rsem,
            device_id={axis: to}, device_id_type=MESH,
        )

    def to_slabs(src, dst, ssem, rsem):
        copies = []
        for k in range(1, slabs):
            to = lax.rem(slab + k, slabs)
            copies.append(remote(src, dst.at[slab], ssem.at[k], rsem.at[k], "slab", to))
        for copy in copies:
            copy.start()
        return copies

    eo[...] = jnp.broadcast_to(sum_ref[...], (8, LANES))
    stress = []
    for side, (z, to) in enumerate(((last, up), (0, down))):
        stress.append(remote(
            st_ref.at[2:5, z], sh.at[side, 0:3], nsend.at[0, 0, side], nrecv.at[0, 0, side], "slab", to
        ))
        stress.append(remote(
            st_ref.at[6, z], sh.at[side, 3], nsend.at[0, 1, side], nrecv.at[0, 1, side], "slab", to
        ))
    for copy in stress:
        copy.start()
    means = to_slabs(eo, mr, rsend.at[0], rrecv.at[0])
    mr[slab] = eo[...]
    moves = []
    for k in range(1, groups):
        to = lax.rem(group + k, groups)
        move = remote(pick_ref.at[to], ab.at[group], bsend.at[k], brecv.at[k], "rve", to)
        move.start()
        moves.append(move)

    def own_planes(z, _):
        c8[z + 1] = st_ref[6, z] * 0.125
        return 0

    lax.fori_loop(0, depth, own_planes, 0)
    ab[group] = pick_ref[group]

    def ydiff(v):
        v = cut(v)
        both = [x - y for x, y in zip(ring_next(v), ring_prev(v))]
        return jnp.concatenate(both, axis=0)

    def xdiff(v):
        return pltpu.roll(v, LANES - 1, 1) - pltpu.roll(v, 1, 1)

    def rhs_plane(z, below, above):
        s3, s4, s5 = st_ref[3, z], st_ref[4, z], st_ref[5, z]
        zd = {c: above(c) - below(c) for c in (2, 3, 4)}
        hr = 0.5 * half_root
        v0 = 0.5 * xdiff(st_ref[0, z]) + hr * (ydiff(s5) + zd[4])
        v1 = hr * (xdiff(s5) + zd[3]) + 0.5 * ydiff(st_ref[1, z])
        v2 = hr * (xdiff(s4) + ydiff(s3)) + 0.5 * zd[2]
        for c, v in enumerate((v0, v1, v2)):
            vv[0, c, z + 1] = v

    def rhs_inner(z, _):
        rhs_plane(z, lambda c: st_ref[c, z - 1], lambda c: st_ref[c, z + 1])
        return 0

    lax.fori_loop(1, last, rhs_inner, 0)
    for copy in stress:
        copy.wait()
    rhs_plane(0, lambda c: sh[0, c - 2], lambda c: st_ref[c, 1])
    rhs_plane(last, lambda c: st_ref[c, last - 1], lambda c: sh[1, c - 2])

    def send_field(j, c):
        first = remote(
            vv.at[j, c, depth], vv.at[j, c, 0], nsend.at[1 + j, c, 0], nrecv.at[1 + j, c, 0], "slab", up
        )
        second = remote(
            vv.at[j, c, 1], vv.at[j, c, depth + 1],
            nsend.at[1 + j, c, 1], nrecv.at[1 + j, c, 1], "slab", down,
        )
        first.start()
        second.start()
        return first, second

    halos = [send_field(0, c) for c in range(3)]
    c8[0] = sh[0, 3] * 0.125
    c8[depth + 1] = sh[1, 3] * 0.125

    for copy in means:
        copy.wait()
    total = mr[0]
    for k in range(1, slabs):
        total = total + mr[k]
    ms[...] = total
    element = []
    for k in range(1, groups):
        to = lax.rem(group + k, groups)
        copy = remote(ms, es.at[group], esend.at[k], erecv.at[k], "rve", to)
        copy.start()
        element.append(copy)
    es[group] = total
    shift = SHIFT * jnp.sum(
        jnp.where(lane_id(1) == MEAN_LANE, total[0:1], 0.0), axis=1, keepdims=True
    )

    def diagonal(z, _):
        wide = spread(cut(c8[z - 1] + 2.0 * c8[z] + c8[z + 1]))
        for i, w in enumerate(wide):
            at = slice(8 * i, 8 * i + 8)
            ee[z, at] = (8.0 * (8.0 + mass_weight) * c8[z, at] - shift) + w
        return 0

    lax.fori_loop(1, depth + 1, diagonal, 0)

    zero = jnp.zeros((8, LANES), jnp.float32)

    def apply_plane(j, c, z, carry):
        norm, curve = carry
        plain, mixed = [], []
        for i in range(0, NVX, 8):
            at = slice(i, i + 8)
            ra, rb, rc = vv[j, c, z - 1, at], vv[j, c, z, at], vv[j, c, z + 1, at]
            crb = c8[z, at] * rb
            plain.append((ra + rc) + (rb + rb))
            mixed.append((c8[z - 1, at] * ra + c8[z + 1, at] * rc) + (crb + crb))
        plain = spread(plain)
        mixed = spread(mixed)
        for i in range(0, NVX, 8):
            at = slice(i, i + 8)
            rb = vv[j, c, z, at]
            image = ee[z, at] * rb - c8[z, at] * plain[i // 8] - mixed[i // 8]
            if j + 1 < ITERS:
                vv[j + 1, c, z, at] = image
            norm = norm + rb * rb
            curve = curve + rb * image
        return norm, curve

    for j in range(ITERS):
        carry = (zero, zero)
        for c in range(3):
            for copy in halos[c]:
                copy.wait()
            carry = apply_plane(j, c, 1, carry)
            carry = apply_plane(j, c, depth, carry)
            if j + 1 < ITERS:
                halos[c] = send_field(j + 1, c)
            carry = lax.fori_loop(2, depth, functools.partial(apply_plane, j, c), carry)
        ps[2 * j : 2 * j + 1] = jnp.sum(carry[0], axis=0, keepdims=True)
        ps[2 * j + 1 : 2 * j + 2] = jnp.sum(carry[1], axis=0, keepdims=True)
    ps[2 * ITERS :] = jnp.zeros((ps.shape[0] - 2 * ITERS, LANES), jnp.float32)

    copies = to_slabs(ps, red, rsend.at[1], rrecv.at[1])
    red[slab] = ps[...]
    for move in moves:
        move.wait()
    for j in range(in_dev):
        source = pg_ref[group, slab * in_dev + j]
        got = ab[source]
        for c in range(7):
            inbox_ref[c, pl.ds(j, BLK // LANES, stride=in_dev), :] = got[c]
    for copy in element:
        copy.wait()
    mine = jnp.zeros((1, LANES), jnp.float32)
    for k in range(groups):
        mine = mine + jnp.where(own_ref[k] == group, es[k][0:1], 0.0)
    elem_ref[...] = mine[:, 0:42]

    for copy in copies:
        copy.wait()
    moments = red[0]
    for k in range(1, slabs):
        moments = moments + red[k]
    moments = jnp.where(lane_id(ps.shape[0]) < NVX, moments, 0.0)
    moments = jnp.sum(moments, axis=1, keepdims=True)
    weights = combine([moments[k : k + 1] for k in range(2 * ITERS)], shift)
    weights = [jnp.broadcast_to(w, (8, LANES)) for w in weights]

    def to_flat(z, _):
        for c in range(3):
            for g in range(NVX // 32):
                rows4 = []
                for r in range(4):
                    at = slice(8 * (4 * g + r), 8 * (4 * g + r) + 8)
                    rows4.append(inner(weights, [vv[j, c, z + 1, at] for j in range(ITERS)]))
                for t, v in enumerate(pack_rows(rows4)):
                    out_ref[c, z, pl.ds(3 * g + t, 8, stride=9)] = v
        return 0

    lax.fori_loop(0, depth, to_flat, 0)


def on_device(
    groups, slabs,
    plastic_strain, hardening_var, strain_start, strain_step, shear_mod, bulk_mod, yield_stress,
    substeps, pull_group, pull_block, owner,
):
    depth = plastic_strain.shape[2]
    in_dev = pull_group.shape[1] // slabs
    volume = float(depth * slabs * PLANE)
    smem = pl.BlockSpec(memory_space=pltpu.SMEM)
    vmem = pl.BlockSpec(memory_space=pltpu.VMEM)
    f32 = jnp.float32
    tiles = PLANE // LANES
    planes = depth // 4 if depth % 4 == 0 else 1
    six = pl.BlockSpec((6, planes, tiles, LANES), lambda i: (0, i, 0, 0))
    one = pl.BlockSpec((planes, tiles, LANES), lambda i: (i, 0, 0))

    def whole(shape):
        return pl.BlockSpec(shape, lambda i: (0,) * len(shape))

    def stay(x):
        return pltpu.with_memory_space_constraint(x, pltpu.HBM)

    def view6(x):
        return stay(x.reshape(6, depth, tiles, LANES))

    def view1(x):
        return stay(x.reshape(depth, tiles, LANES))

    pick_shape = (groups, 7, BLK // LANES, LANES)
    shapes = ((7, depth, NVX, LANES), pick_shape, (1, LANES))
    stress, picked, partial_sums = pl.pallas_call(
        functools.partial(material_kernel, depth, volume, in_dev, planes),
        grid=(depth // planes,),
        in_specs=[smem, smem, smem, six, one, six, six, one, one, one],
        out_specs=[
            pl.BlockSpec((7, planes, NVX, LANES), lambda i: (0, i, 0, 0)),
            whole(shapes[1]),
            whole(shapes[2]),
        ],
        out_shape=[jax.ShapeDtypeStruct(s, f32) for s in shapes],
        scratch_shapes=[
            pltpu.VMEM((8 + len(PAIRS), 8, LANES), f32),
            pltpu.VMEM((7, planes, tiles, LANES), f32),
            pltpu.VMEM((tiles, LANES), jnp.int32),
            pltpu.VMEM((5, tiles, LANES), f32),
            pltpu.VMEM((5, tiles, LANES), f32),
            pltpu.VMEM((tiles, LANES), f32),
            pltpu.VMEM((tiles, LANES), f32),
            pltpu.VMEM((7, tiles, LANES), f32),
        ],
        compiler_params=pltpu.CompilerParams(
            dimension_semantics=("arbitrary",), vmem_limit_bytes=16 * 1024 * 1024
        ),
        name="material",
    )(
        substeps, pull_group, pull_block, view6(plastic_strain), view1(hardening_var),
        view6(strain_start), view6(strain_step), view1(shear_mod), view1(bulk_mod),
        view1(yield_stress),
    )
    plane = (NVX, LANES)
    dma = pltpu.SemaphoreType.DMA
    correction, inbox, element_sums = pl.pallas_call(
        functools.partial(solve_kernel, depth, groups, slabs, in_dev),
        in_specs=[smem, smem, vmem, vmem, vmem],
        out_specs=[vmem, vmem, vmem],
        out_shape=[
            jax.ShapeDtypeStruct((3, depth, tiles, LANES), f32),
            jax.ShapeDtypeStruct((7, in_dev * BLK // LANES, LANES), f32),
            jax.ShapeDtypeStruct((1, 42), f32),
        ],
        scratch_shapes=[
            pltpu.VMEM((2, 4) + plane, f32),
            pltpu.VMEM((depth + 2,) + plane, f32),
            pltpu.VMEM((depth + 2,) + plane, f32),
            pltpu.VMEM((ITERS, 3, depth + 2) + plane, f32),
            pltpu.VMEM((16, LANES), f32),
            pltpu.VMEM((slabs, 16, LANES), f32),
            pltpu.VMEM((8, LANES), f32),
            pltpu.VMEM((slabs, 8, LANES), f32),
            pltpu.VMEM(pick_shape, f32),
            pltpu.VMEM((groups, 8, LANES), f32),
            pltpu.VMEM((8, LANES), f32),
            dma((ITERS + 1, 3, 2)),
            dma((ITERS + 1, 3, 2)),
            dma((2, slabs)),
            dma((2, slabs)),
            dma((groups,)),
            dma((groups,)),
            dma((groups,)),
            dma((groups,)),
        ],
        compiler_params=pltpu.CompilerParams(
            collective_id=0, has_side_effects=True, vmem_limit_bytes=26 * 1024 * 1024
        ),
        name="solve",
    )(pull_group, owner, stress, picked, partial_sums)
    correction = correction.reshape(3, 1, depth, PLANE)
    inbox = inbox.reshape(7, BLK // LANES, in_dev, LANES).swapaxes(1, 2)
    return correction, inbox.reshape(7, 1, in_dev, BLK), element_sums


def solution(mesh):
    return jax.shard_map(
        functools.partial(on_device, mesh.shape["rve"], mesh.shape["slab"]),
        mesh=mesh,
        in_specs=(
            P(None, "rve", "slab", None),
            P("rve", "slab", None),
            P(None, "rve", "slab", None),
            P(None, "rve", "slab", None),
            P("rve", "slab", None),
            P("rve", "slab", None),
            P("rve", "slab", None),
            P(),
            P(),
            P(),
            P(),
        ),
        out_specs=(P(None, "rve", "slab", None), P(None, "rve", "slab", None), P("rve", None)),
        check_vma=False,
    )
```

```python
import functools
import math

import jax
import jax.numpy as jnp
from jax import lax
from jax.experimental import pallas as pl
from jax.experimental.pallas import tpu as pltpu
from jax.sharding import PartitionSpec as P

NVX = 96
ITERS = 5
SUBMAX = 8
PLANE = 9216
BLK = 2304
LANES = 128
PART = 24
MEAN_LANE = 42
SHIFT = 12.0
MESH = pl.DeviceIdType.MESH

hard_ratio = 0.3
mass_weight = 0.05
root_two_thirds = math.sqrt(2.0 / 3.0)
half_root = 1.0 / math.sqrt(2.0)
KEPT = (0, 1, 3, 4, 5)
PAIRS = tuple((i, j) for i in range(5) for j in range(i, 5))


def lane_id(rows):
    return lax.broadcasted_iota(jnp.int32, (rows, LANES), 1)


def unpack_rows(a, b, c):
    lane = lane_id(a.shape[0])
    plain = (
        a,
        pltpu.roll(jnp.where(lane >= 96, a, b), 32, 1),
        pltpu.roll(jnp.where(lane >= 64, b, c), 64, 1),
        pltpu.roll(c, 96, 1),
    )
    out = []
    for row in plain:
        halo = jnp.where(lane < 112, pltpu.roll(row, 96, 1), pltpu.roll(row, 32, 1))
        out.append(jnp.where(lane < 96, row, halo))
    return out


def pack_rows(rows4):
    t0, t1, t2, t3 = rows4
    lane = lane_id(t0.shape[0])
    r1, r2, r3 = pltpu.roll(t1, 96, 1), pltpu.roll(t2, 64, 1), pltpu.roll(t3, 32, 1)
    return (
        jnp.where(lane < 96, t0, r1),
        jnp.where(lane < 64, r1, r2),
        jnp.where(lane < 32, r2, r3),
    )


def norm_form(a, b):
    return (
        a[0] * (b[0] + b[0] + b[1]) + a[1] * (b[0] + b[1] + b[1])
        + a[2] * b[2] + a[3] * b[3] + a[4] * b[4]
    )


def deviator(vals):
    trace = vals[0] + vals[1] + vals[2]
    third = trace * (1.0 / 3.0)
    return [vals[0] - third, vals[1] - third, vals[3], vals[4], vals[5]], trace


def full(five):
    return [five[0], five[1], -(five[0] + five[1]), five[2], five[3], five[4]]


def material_plane(z, counts, ins, st_ref, acc_ref, hist_ref, tmp_ref):
    p_ref, h_ref, b_ref, d_ref, g_ref, k_ref, y_ref = ins
    tiles = PLANE // LANES
    parts = tuple(slice(t, t + PART) for t in range(0, tiles, PART))
    quarter_rows = BLK // LANES

    def strains(rows):
        dev0, tr0 = deviator([b_ref[c, z, rows] - p_ref[c, z, rows] for c in range(6)])
        devs, trs = deviator([d_ref[c, z, rows] for c in range(6)])
        return dev0, devs, tr0 + trs

    state = []
    for rows in parts:
        row = lax.broadcasted_iota(jnp.int32, (PART, LANES), 0) + rows.start
        count = jnp.full((PART, LANES), counts[0], jnp.int32)
        for q in range(1, 4):
            count = jnp.where(row >= q * quarter_rows, counts[q], count)
        count = count.astype(jnp.float32)
        inv = 1.0 / count
        dev0, devs, _ = strains(rows)
        s00 = norm_form(dev0, dev0)
        s01 = 2.0 * inv * norm_form(dev0, devs)
        s11 = inv * inv * norm_form(devs, devs)
        level = (11.0 * root_two_thirds / 2.2) * (
            y_ref[z, rows] / g_ref[z, rows] + hard_ratio * h_ref[z, rows]
        )
        state.append([jnp.ones_like(inv), count - float(SUBMAX), level, level, s00, s01, s11, inv])
    for turn in range(SUBMAX - 1):
        for one in state:
            a, b, level, _, s00, s01, s11, _ = one
            b = b + 1.0
            square = jnp.maximum(a * (a * s00 + b * s01) + (b * b) * s11, 1e-30)
            rs = lax.rsqrt(square)
            fac = jnp.minimum((1.0 + level * rs) * (1.0 / 11.0), 1.0)
            fac = jnp.where(b > 0.0, fac, 1.0)
            one[2] = level + (1.0 - fac) * (square * rs)
            one[0] = a * fac
            one[1] = b * fac
    sums = [None] * (8 + len(PAIRS))
    for rows, one in zip(parts, state):
        a, b, level, level0, _, _, _, inv = one
        b = (b + 1.0) * inv
        dev0, devs, trace = strains(rows)
        dd = [a * x + b * y for x, y in zip(dev0, devs)]
        square = jnp.maximum(norm_form(dd, dd), 1e-30)
        rs = lax.rsqrt(square)
        fac = jnp.minimum((1.0 + level * rs) * (1.0 / 11.0), 1.0)
        level = level + (1.0 - fac) * (square * rs)
        fin = [fac * v for v in dd]
        mu = g_ref[z, rows]
        coef = mu * fac
        weight = (coef - mu) * (rs * rs)
        bulk = k_ref[z, rows]
        vol = bulk * trace
        two_mu = 2.0 * mu
        ms = [two_mu * v for v in fin]
        wn = [weight * v for v in dd]
        gone = full([x + y - w for x, y, w in zip(dev0, devs, fin)])
        for c, v in enumerate(full(ms)):
            tmp_ref[c, rows] = v + vol if c < 3 else v
            hist_ref[c, z, rows] = p_ref[c, z, rows] + gone[c]
        tmp_ref[6, rows] = coef
        hist_ref[6, z, rows] = h_ref[z, rows] + root_two_thirds * (level - level0)
        terms = [vol, bulk, coef] + ms + [wn[i] * dd[j] for i, j in PAIRS]
        for t, v in enumerate(terms):
            for o in range(0, PART, 8):
                piece = v[o : o + 8]
                sums[t] = piece if sums[t] is None else sums[t] + piece
    for t, v in enumerate(sums):
        acc_ref[t] += v
    for f in range(7):
        for g in range(tiles // 24):
            a, b, c = (tmp_ref[f, pl.ds(3 * g + k, 8, stride=9)] for k in range(3))
            for r, rowv in enumerate(unpack_rows(a, b, c)):
                at = 8 * (4 * g + r)
                st_ref[f, z, at : at + 8] = rowv


def summary_row(acc_ref, volume):
    tot = [
        jnp.sum(acc_ref[t], axis=(0, 1), keepdims=True) * (1.0 / volume)
        for t in range(8 + len(PAIRS))
    ]
    vol, bulk, coef = tot[0], tot[1], tot[2]
    ms = tot[3:8]
    stress = [vol + ms[0], vol + ms[1], vol - ms[0] - ms[1], ms[2], ms[3], ms[4]]
    table = {}
    for t, (i, j) in enumerate(PAIRS):
        table[(KEPT[i], KEPT[j])] = tot[8 + t]
        table[(KEPT[j], KEPT[i])] = tot[8 + t]
    for j in KEPT:
        table[(2, j)] = -(table[(0, j)] + table[(1, j)])
        table[(j, 2)] = table[(2, j)]
    table[(2, 2)] = -(table[(2, 0)] + table[(2, 1)])
    lane = lane_id(1)
    row = jnp.zeros((1, LANES), jnp.float32)
    for c in range(6):
        row = jnp.where(lane == c, stress[c], row)
    for i in range(6):
        for j in range(6):
            v = 2.0 * table[(i, j)]
            if i == j:
                v = v + 2.0 * coef
            if i < 3 and j < 3:
                v = v + bulk - (2.0 / 3.0) * coef
            row = jnp.where(lane == 6 + 6 * i + j, v, row)
    return jnp.where(lane == MEAN_LANE, coef, row)


def ring_next(pieces):
    return pieces[1:] + [pltpu.roll(pieces[0], 7, 0)]


def ring_prev(pieces):
    return [pltpu.roll(pieces[-1], 1, 0)] + pieces[:-1]


def cut(v):
    return [v[i : i + 8] for i in range(0, NVX, 8)]


def spread(pieces):
    p = [x + y for x, y in zip(pieces, ring_next(pieces))]
    p = [x + y for x, y in zip(p, ring_prev(p))]
    left = [pltpu.roll(x, LANES - 1, 1) for x in p]
    right = [pltpu.roll(x, 1, 1) for x in p]
    return [(x + x) + (y + w) for x, y, w in zip(p, left, right)]


def tree(values):
    while len(values) > 1:
        pairs = [x + y for x, y in zip(values[::2], values[1::2])]
        values = pairs + values[2 * len(pairs) :]
    return values[0]


def inner(a, b):
    total = a[0] * b[0]
    for x, y in zip(a[1:], b[1:]):
        total = total + x * y
    return total


def combine(moments, shift):
    one = jnp.ones_like(moments[0])
    res_c, dir_c, out = [one], [one], []
    res_m, dir_m = list(moments), list(moments)
    norm = moments[0]
    for turn in range(ITERS):
        image_m = [shift * x + y for x, y in zip(dir_m, dir_m[1:])]
        alpha = norm / inner(dir_c, image_m)
        grown = out + [jnp.zeros_like(one)]
        out = [x + alpha * y for x, y in zip(grown, dir_c)]
        if turn == ITERS - 1:
            return out
        image_c = [shift * dir_c[0]]
        image_c += [shift * x + y for x, y in zip(dir_c[1:], dir_c)] + [dir_c[-1]]
        res_c = [x - alpha * y for x, y in zip(res_c, image_c)] + [-alpha * image_c[-1]]
        res_m = [x - alpha * y for x, y in zip(res_m, image_m)]
        norm_next = inner(res_c, res_m)
        beta = norm_next / norm
        norm = norm_next
        dir_c = [x + beta * y for x, y in zip(res_c, dir_c)] + [res_c[-1]]
        dir_m = [x + beta * y for x, y in zip(res_m, dir_m)]


def rve_kernel(
    depth, groups, slabs, in_dev, volume,
    sub_in, pg_in, pb_in, own_in, p_in, h_in, b_in, d_in, g_in, k_in, y_in,
    out_ref, inbox_ref, elem_ref,
    sub_ref, pg_ref, pb_ref, own_ref,
    p_ref, h_ref, b_ref, d_ref, g_ref, k_ref, y_ref,
    st_ref, acc_ref, hist_ref, tmp_ref, pick_ref,
    sh, c8, ee, v0, v1, v2, v3, v4, ps, red, ms, mr, ab, es, eo,
    insem, smallsem,
    nsend, nrecv, rsend, rrecv, bsend, brecv, esend, erecv,
):
    group = lax.axis_index("rve")
    slab = lax.axis_index("slab")
    up = lax.rem(slab + 1, slabs)
    down = lax.rem(slab + slabs - 1, slabs)
    last = depth - 1
    vv = (v0, v1, v2, v3, v4)
    ins = (p_ref, h_ref, b_ref, d_ref, g_ref, k_ref, y_ref)
    sources = (p_in, h_in, b_in, d_in, g_in, k_in, y_in)

    def fetch(z, k):
        wide = len(ins[k].shape) == 4
        return pltpu.make_async_copy(
            sources[k].at[:, z] if wide else sources[k].at[z],
            ins[k].at[:, z] if wide else ins[k].at[z],
            insem.at[z, k],
        )

    small = [
        pltpu.make_async_copy(src, dst, smallsem.at[i])
        for i, (src, dst) in enumerate(
            ((sub_in, sub_ref), (pg_in, pg_ref), (pb_in, pb_ref), (own_in, own_ref))
        )
    ]
    small[0].start()
    for z in (0, last):
        for k in range(7):
            fetch(z, k).start()
    for copy in small[1:]:
        copy.start()

    def fetch_plane(z, _):
        for k in range(7):
            fetch(z, k).start()
        return 0

    lax.fori_loop(1, last, fetch_plane, 0)
    barrier = pltpu.get_barrier_semaphore()
    for k in range(1, slabs):
        pl.semaphore_signal(
            barrier, inc=1, device_id={"slab": lax.rem(slab + k, slabs)}, device_id_type=MESH
        )
    for k in range(1, groups):
        pl.semaphore_signal(
            barrier, inc=1, device_id={"rve": lax.rem(group + k, groups)}, device_id_type=MESH
        )

    def remote(src, dst, ssem, rsem, axis, to):
        return pltpu.make_async_remote_copy(
            src_ref=src, dst_ref=dst, send_sem=ssem, recv_sem=rsem,
            device_id={axis: to}, device_id_type=MESH,
        )

    def to_slabs(src, dst, ssem, rsem):
        copies = []
        for k in range(1, slabs):
            to = lax.rem(slab + k, slabs)
            copies.append(remote(src, dst.at[slab], ssem.at[k], rsem.at[k], "slab", to))
        for copy in copies:
            copy.start()
        return copies

    acc_ref[...] = jnp.zeros_like(acc_ref)
    small[0].wait()

    def material(z):
        for k in range(7):
            fetch(z, k).wait()
        base = (slab * depth + z) * 4
        counts = [sub_ref[group, base + q] for q in range(4)]
        material_plane(z, counts, ins, st_ref, acc_ref, hist_ref, tmp_ref)
        c8[z + 1] = st_ref[6, z] * 0.125

    def material_edge(i, _):
        material(i * last)
        return 0

    def material_inner(z, _):
        material(z)
        return 0

    lax.fori_loop(0, 2, material_edge, 0)
    pl.semaphore_wait(barrier, slabs + groups - 2)
    stress = []
    for side, (z, to) in enumerate(((last, up), (0, down))):
        stress.append(remote(
            st_ref.at[2:5, z], sh.at[side, 0:3], nsend.at[0, 0, side], nrecv.at[0, 0, side], "slab", to
        ))
        stress.append(remote(
            st_ref.at[6, z], sh.at[side, 3], nsend.at[0, 1, side], nrecv.at[0, 1, side], "slab", to
        ))
    for copy in stress:
        copy.start()
    lax.fori_loop(1, last, material_inner, 0)
    eo[...] = jnp.broadcast_to(summary_row(acc_ref, volume), (8, LANES))
    means = to_slabs(eo, mr, rsend.at[0], rrecv.at[0])
    mr[slab] = eo[...]
    for copy in small[1:]:
        copy.wait()
    quarter_rows = BLK // LANES
    for g in range(groups):
        chosen = slab * (4 * depth)
        for j in range(in_dev):
            slot = slab * in_dev + j
            chosen = jnp.where(pg_ref[g, slot] == group, pb_ref[g, slot], chosen)
        chosen = jnp.clip(chosen - slab * (4 * depth), 0, 4 * depth - 1)
        z = chosen // 4
        quarter = chosen - 4 * z
        for c in range(7):
            plane = hist_ref[c, z]
            got = plane[0:quarter_rows]
            for q in range(1, 4):
                got = jnp.where(quarter == q, plane[q * quarter_rows : (q + 1) * quarter_rows], got)
            pick_ref[g, c] = got
    moves = []
    for k in range(1, groups):
        to = lax.rem(group + k, groups)
        move = remote(pick_ref.at[to], ab.at[group], bsend.at[k], brecv.at[k], "rve", to)
        move.start()
        moves.append(move)
    ab[group] = pick_ref[group]

    def ydiff(v):
        v = cut(v)
        both = [x - y for x, y in zip(ring_next(v), ring_prev(v))]
        return jnp.concatenate(both, axis=0)

    def xdiff(v):
        return pltpu.roll(v, LANES - 1, 1) - pltpu.roll(v, 1, 1)

    def rhs_plane(z, below, above):
        s3, s4, s5 = st_ref[3, z], st_ref[4, z], st_ref[5, z]
        zd = {c: above(c) - below(c) for c in (2, 3, 4)}
        hr = 0.5 * half_root
        f0 = 0.5 * xdiff(st_ref[0, z]) + hr * (ydiff(s5) + zd[4])
        f1 = hr * (xdiff(s5) + zd[3]) + 0.5 * ydiff(st_ref[1, z])
        f2 = hr * (xdiff(s4) + ydiff(s3)) + 0.5 * zd[2]
        for c, v in enumerate((f0, f1, f2)):
            v0[c, z + 1] = v

    def rhs_inner(z, _):
        rhs_plane(z, lambda c: st_ref[c, z - 1], lambda c: st_ref[c, z + 1])
        return 0

    lax.fori_loop(1, last, rhs_inner, 0, unroll=2)
    for copy in stress:
        copy.wait()
    rhs_plane(0, lambda c: sh[0, c - 2], lambda c: st_ref[c, 1])
    rhs_plane(last, lambda c: st_ref[c, last - 1], lambda c: sh[1, c - 2])

    def send_field(j, c):
        first = remote(
            vv[j].at[c, depth], vv[j].at[c, 0], nsend.at[1 + j, c, 0], nrecv.at[1 + j, c, 0], "slab", up
        )
        second = remote(
            vv[j].at[c, 1], vv[j].at[c, depth + 1],
            nsend.at[1 + j, c, 1], nrecv.at[1 + j, c, 1], "slab", down,
        )
        first.start()
        second.start()
        return first, second

    halos = [send_field(0, c) for c in range(3)]
    c8[0] = sh[0, 3] * 0.125
    c8[depth + 1] = sh[1, 3] * 0.125

    for copy in means:
        copy.wait()
    total = mr[0]
    for k in range(1, slabs):
        total = total + mr[k]
    ms[...] = total
    element = []
    for k in range(1, groups):
        to = lax.rem(group + k, groups)
        copy = remote(ms, es.at[group], esend.at[k], erecv.at[k], "rve", to)
        copy.start()
        element.append(copy)
    es[group] = total
    shift = SHIFT * jnp.sum(
        jnp.where(lane_id(1) == MEAN_LANE, total[0:1], 0.0), axis=1, keepdims=True
    )

    def diagonal(z, _):
        wide = spread(cut(c8[z - 1] + 2.0 * c8[z] + c8[z + 1]))
        for i, w in enumerate(wide):
            at = slice(8 * i, 8 * i + 8)
            ee[z, at] = (8.0 * (8.0 + mass_weight) * c8[z, at] - shift) + w
        return 0

    lax.fori_loop(1, depth + 1, diagonal, 0, unroll=3)

    zero = jnp.zeros((8, LANES), jnp.float32)

    def apply_plane(j, c, z, carry):
        norm, curve = carry
        plain, mixed, norms, curves = [], [], [], []
        for i in range(0, NVX, 8):
            at = slice(i, i + 8)
            ra, rb, rc = vv[j][c, z - 1, at], vv[j][c, z, at], vv[j][c, z + 1, at]
            crb = c8[z, at] * rb
            plain.append((ra + rc) + (rb + rb))
            mixed.append((c8[z - 1, at] * ra + c8[z + 1, at] * rc) + (crb + crb))
        plain = spread(plain)
        mixed = spread(mixed)
        for i in range(0, NVX, 8):
            at = slice(i, i + 8)
            rb = vv[j][c, z, at]
            image = ee[z, at] * rb - c8[z, at] * plain[i // 8] - mixed[i // 8]
            if j + 1 < ITERS:
                vv[j + 1][c, z, at] = image
            norms.append(rb * rb)
            curves.append(rb * image)
        return norm + tree(norms), curve + tree(curves)

    for j in range(ITERS):
        carry = (zero, zero)
        for c in range(3):
            for copy in halos[c]:
                copy.wait()
            carry = apply_plane(j, c, 1, carry)
            carry = apply_plane(j, c, depth, carry)
            if j + 1 < ITERS:
                halos[c] = send_field(j + 1, c)
            carry = lax.fori_loop(2, depth, functools.partial(apply_plane, j, c), carry, unroll=5)
        ps[2 * j : 2 * j + 1] = jnp.sum(carry[0], axis=0, keepdims=True)
        ps[2 * j + 1 : 2 * j + 2] = jnp.sum(carry[1], axis=0, keepdims=True)
    ps[2 * ITERS :] = jnp.zeros((ps.shape[0] - 2 * ITERS, LANES), jnp.float32)

    copies = to_slabs(ps, red, rsend.at[1], rrecv.at[1])
    red[slab] = ps[...]
    for move in moves:
        move.wait()
    for j in range(in_dev):
        source = pg_ref[group, slab * in_dev + j]
        got = ab[jnp.clip(source, 0, groups - 1)]
        for c in range(7):
            inbox_ref[c, pl.ds(j, BLK // LANES, stride=in_dev), :] = got[c]
    for copy in element:
        copy.wait()
    mine = jnp.zeros((1, LANES), jnp.float32)
    for k in range(groups):
        mine = mine + jnp.where(own_ref[k] == group, es[k][0:1], 0.0)
    elem_ref[...] = mine[:, 0:42]

    for copy in copies:
        copy.wait()
    moments = red[0]
    for k in range(1, slabs):
        moments = moments + red[k]
    moments = jnp.where(lane_id(ps.shape[0]) < NVX, moments, 0.0)
    moments = jnp.sum(moments, axis=1, keepdims=True)
    weights = combine([moments[k : k + 1] for k in range(2 * ITERS)], shift)
    weights = [jnp.broadcast_to(w, (8, LANES)) for w in weights]

    def to_flat(z, _):
        for c in range(3):
            for g in range(NVX // 32):
                rows4 = []
                for r in range(4):
                    at = slice(8 * (4 * g + r), 8 * (4 * g + r) + 8)
                    rows4.append(inner(weights, [vv[j][c, z + 1, at] for j in range(ITERS)]))
                for t, v in enumerate(pack_rows(rows4)):
                    out_ref[c, z, pl.ds(3 * g + t, 8, stride=9)] = v
        return 0

    lax.fori_loop(0, depth, to_flat, 0, unroll=2)


def on_device(
    groups, slabs,
    plastic_strain, hardening_var, strain_start, strain_step, shear_mod, bulk_mod, yield_stress,
    substeps, pull_group, pull_block, owner,
):
    depth = plastic_strain.shape[2]
    in_dev = pull_group.shape[1] // slabs
    volume = float(depth * slabs * PLANE)
    vmem = pl.BlockSpec(memory_space=pltpu.VMEM)
    hbm = pl.BlockSpec(memory_space=pl.ANY)
    f32 = jnp.float32
    tiles = PLANE // LANES

    def stay(x):
        return pltpu.with_memory_space_constraint(x, pltpu.HBM)

    def view6(x):
        return stay(x.reshape(6, depth, tiles, LANES))

    def view1(x):
        return stay(x.reshape(depth, tiles, LANES))

    pick_shape = (groups, 7, BLK // LANES, LANES)
    plane = (NVX, LANES)
    flat = (tiles, LANES)
    dma = pltpu.SemaphoreType.DMA
    ints = [pltpu.SMEM(x.shape, jnp.int32) for x in (substeps, pull_group, pull_block, owner)]
    six, one = pltpu.VMEM((6, depth) + flat, f32), pltpu.VMEM((depth,) + flat, f32)
    correction, inbox, element_sums = pl.pallas_call(
        functools.partial(rve_kernel, depth, groups, slabs, in_dev, volume),
        in_specs=[hbm] * 11,
        out_specs=[vmem, vmem, vmem],
        out_shape=[
            jax.ShapeDtypeStruct((3, depth, tiles, LANES), f32),
            jax.ShapeDtypeStruct((7, in_dev * BLK // LANES, LANES), f32),
            jax.ShapeDtypeStruct((1, 42), f32),
        ],
        scratch_shapes=[
            *ints,
            six, one, six, six, one, one, one,
            pltpu.VMEM((7, depth) + plane, f32),
            pltpu.VMEM((8 + len(PAIRS), 8, LANES), f32),
            pltpu.VMEM((7, depth) + flat, f32),
            pltpu.VMEM((7,) + flat, f32),
            pltpu.VMEM(pick_shape, f32),
            pltpu.VMEM((2, 4) + plane, f32),
            pltpu.VMEM((depth + 2,) + plane, f32),
            pltpu.VMEM((depth + 2,) + plane, f32),
            *[pltpu.VMEM((3, depth + 2) + plane, f32)] * ITERS,
            pltpu.VMEM((16, LANES), f32),
            pltpu.VMEM((slabs, 16, LANES), f32),
            pltpu.VMEM((8, LANES), f32),
            pltpu.VMEM((slabs, 8, LANES), f32),
            pltpu.VMEM(pick_shape, f32),
            pltpu.VMEM((groups, 8, LANES), f32),
            pltpu.VMEM((8, LANES), f32),
            dma((depth, 7)),
            dma((4,)),
            dma((ITERS + 1, 3, 2)),
            dma((ITERS + 1, 3, 2)),
            dma((2, slabs)),
            dma((2, slabs)),
            dma((groups,)),
            dma((groups,)),
            dma((groups,)),
            dma((groups,)),
        ],
        compiler_params=pltpu.CompilerParams(
            collective_id=0, has_side_effects=True, vmem_limit_bytes=48 * 1024 * 1024
        ),
        name="rve_step",
    )(
        stay(substeps), stay(pull_group), stay(pull_block), stay(owner),
        view6(plastic_strain), view1(hardening_var), view6(strain_start), view6(strain_step),
        view1(shear_mod), view1(bulk_mod), view1(yield_stress),
    )
    correction = correction.reshape(3, 1, depth, PLANE)
    inbox = inbox.reshape(7, BLK // LANES, in_dev, LANES).swapaxes(1, 2)
    return correction, inbox.reshape(7, 1, in_dev, BLK), element_sums


def solution(mesh):
    return jax.shard_map(
        functools.partial(on_device, mesh.shape["rve"], mesh.shape["slab"]),
        mesh=mesh,
        in_specs=(
            P(None, "rve", "slab", None),
            P("rve", "slab", None),
            P(None, "rve", "slab", None),
            P(None, "rve", "slab", None),
            P("rve", "slab", None),
            P("rve", "slab", None),
            P("rve", "slab", None),
            P(),
            P(),
            P(),
            P(),
        ),
        out_specs=(P(None, "rve", "slab", None), P(None, "rve", "slab", None), P("rve", None)),
        check_vma=False,
    )
```

```python
import functools
import math

import jax
import jax.numpy as jnp
from jax import lax
from jax.experimental import pallas as pl
from jax.experimental.pallas import tpu as pltpu
from jax.sharding import PartitionSpec as P

NVX = 96
ITERS = 5
SUBMAX = 8
PLANE = 9216
BLK = 2304
LANES = 128
PART = 24
MEAN_LANE = 42
SHIFT = 12.0
MESH = pl.DeviceIdType.MESH

hard_ratio = 0.3
mass_weight = 0.05
root_two_thirds = math.sqrt(2.0 / 3.0)
half_root = 1.0 / math.sqrt(2.0)
KEPT = (0, 1, 3, 4, 5)
PAIRS = tuple((i, j) for i in range(5) for j in range(i, 5))


def lane_id(rows):
    return lax.broadcasted_iota(jnp.int32, (rows, LANES), 1)


def unpack_rows(a, b, c):
    lane = lane_id(a.shape[0])
    plain = (
        a,
        pltpu.roll(jnp.where(lane >= 96, a, b), 32, 1),
        pltpu.roll(jnp.where(lane >= 64, b, c), 64, 1),
        pltpu.roll(c, 96, 1),
    )
    return plain


def pack_rows(rows4):
    t0, t1, t2, t3 = rows4
    lane = lane_id(t0.shape[0])
    r1, r2, r3 = pltpu.roll(t1, 96, 1), pltpu.roll(t2, 64, 1), pltpu.roll(t3, 32, 1)
    return (
        jnp.where(lane < 96, t0, r1),
        jnp.where(lane < 64, r1, r2),
        jnp.where(lane < 32, r2, r3),
    )


def norm_form(a, b):
    return (
        a[0] * (b[0] + b[0] + b[1]) + a[1] * (b[0] + b[1] + b[1])
        + a[2] * b[2] + a[3] * b[3] + a[4] * b[4]
    )


def deviator(vals):
    trace = vals[0] + vals[1] + vals[2]
    third = trace * (1.0 / 3.0)
    return [vals[0] - third, vals[1] - third, vals[3], vals[4], vals[5]], trace


def full(five):
    return [five[0], five[1], -(five[0] + five[1]), five[2], five[3], five[4]]


def material_plane(z, counts, ins, st_ref, acc_ref, hist_ref, tmp_ref):
    p_ref, h_ref, b_ref, d_ref, g_ref, k_ref, y_ref = ins
    tiles = PLANE // LANES
    parts = tuple(slice(t, t + PART) for t in range(0, tiles, PART))
    quarter_rows = BLK // LANES

    def strains(rows):
        dev0, tr0 = deviator([b_ref[c, z, rows] - p_ref[c, z, rows] for c in range(6)])
        devs, trs = deviator([d_ref[c, z, rows] for c in range(6)])
        return dev0, devs, tr0 + trs

    state = []
    for rows in parts:
        row = lax.broadcasted_iota(jnp.int32, (PART, LANES), 0) + rows.start
        count = jnp.full((PART, LANES), counts[0], jnp.int32)
        for q in range(1, 4):
            count = jnp.where(row >= q * quarter_rows, counts[q], count)
        count = count.astype(jnp.float32)
        inv = 1.0 / count
        dev0, devs, _ = strains(rows)
        s00 = norm_form(dev0, dev0)
        s01 = 2.0 * inv * norm_form(dev0, devs)
        s11 = inv * inv * norm_form(devs, devs)
        level = (11.0 * root_two_thirds / 2.2) * (
            y_ref[z, rows] / g_ref[z, rows] + hard_ratio * h_ref[z, rows]
        )
        state.append([jnp.ones_like(inv), count - float(SUBMAX), level, level, s00, s01, s11, inv])
    for turn in range(SUBMAX - 1):
        for one in state:
            a, b, level, _, s00, s01, s11, _ = one
            b = b + 1.0
            square = jnp.maximum(a * (a * s00 + b * s01) + (b * b) * s11, 1e-30)
            rs = lax.rsqrt(square)
            fac = jnp.minimum((1.0 + level * rs) * (1.0 / 11.0), 1.0)
            fac = jnp.where(b > 0.0, fac, 1.0)
            one[2] = level + (1.0 - fac) * (square * rs)
            one[0] = a * fac
            one[1] = b * fac
    sums = [None] * (8 + len(PAIRS))
    for rows, one in zip(parts, state):
        a, b, level, level0, _, _, _, inv = one
        b = (b + 1.0) * inv
        dev0, devs, trace = strains(rows)
        dd = [a * x + b * y for x, y in zip(dev0, devs)]
        square = jnp.maximum(norm_form(dd, dd), 1e-30)
        rs = lax.rsqrt(square)
        fac = jnp.minimum((1.0 + level * rs) * (1.0 / 11.0), 1.0)
        level = level + (1.0 - fac) * (square * rs)
        fin = [fac * v for v in dd]
        mu = g_ref[z, rows]
        coef = mu * fac
        weight = (coef - mu) * (rs * rs)
        bulk = k_ref[z, rows]
        vol = bulk * trace
        two_mu = 2.0 * mu
        ms = [two_mu * v for v in fin]
        wn = [weight * v for v in dd]
        gone = full([x + y - w for x, y, w in zip(dev0, devs, fin)])
        for c, v in enumerate(full(ms)):
            tmp_ref[c, rows] = v + vol if c < 3 else v
            hist_ref[c, z, rows] = p_ref[c, z, rows] + gone[c]
        tmp_ref[6, rows] = coef
        hist_ref[6, z, rows] = h_ref[z, rows] + root_two_thirds * (level - level0)
        terms = [vol, bulk, coef] + ms + [wn[i] * dd[j] for i, j in PAIRS]
        for t, v in enumerate(terms):
            for o in range(0, PART, 8):
                piece = v[o : o + 8]
                sums[t] = piece if sums[t] is None else sums[t] + piece
    for t, v in enumerate(sums):
        acc_ref[t] += v
    for f in range(7):
        for g in range(tiles // 24):
            a, b, c = (tmp_ref[f, pl.ds(3 * g + k, 8, stride=9)] for k in range(3))
            for r, rowv in enumerate(unpack_rows(a, b, c)):
                at = 8 * (4 * g + r)
                st_ref[f, z, at : at + 8] = rowv


def summary_row(acc_ref, volume):
    tot = [
        jnp.sum(acc_ref[t], axis=(0, 1), keepdims=True) * (1.0 / volume)
        for t in range(8 + len(PAIRS))
    ]
    vol, bulk, coef = tot[0], tot[1], tot[2]
    ms = tot[3:8]
    stress = [vol + ms[0], vol + ms[1], vol - ms[0] - ms[1], ms[2], ms[3], ms[4]]
    table = {}
    for t, (i, j) in enumerate(PAIRS):
        table[(KEPT[i], KEPT[j])] = tot[8 + t]
        table[(KEPT[j], KEPT[i])] = tot[8 + t]
    for j in KEPT:
        table[(2, j)] = -(table[(0, j)] + table[(1, j)])
        table[(j, 2)] = table[(2, j)]
    table[(2, 2)] = -(table[(2, 0)] + table[(2, 1)])
    lane = lane_id(1)
    row = jnp.zeros((1, LANES), jnp.float32)
    for c in range(6):
        row = jnp.where(lane == c, stress[c], row)
    for i in range(6):
        for j in range(6):
            v = 2.0 * table[(i, j)]
            if i == j:
                v = v + 2.0 * coef
            if i < 3 and j < 3:
                v = v + bulk - (2.0 / 3.0) * coef
            row = jnp.where(lane == 6 + 6 * i + j, v, row)
    return jnp.where(lane == MEAN_LANE, coef, row)


def ring_next(pieces):
    return pieces[1:] + [pltpu.roll(pieces[0], 7, 0)]


def ring_prev(pieces):
    return [pltpu.roll(pieces[-1], 1, 0)] + pieces[:-1]


def cut(v):
    return [v[i : i + 8] for i in range(0, v.shape[0], 8)]


def fold(pieces):
    lane = lane_id(8)
    return [
        jnp.where(lane < NVX, pieces[i], pltpu.roll(pieces[9 + i // 3], 96 - 32 * (i % 3), 1))
        for i in range(9)
    ]


def unfold(pieces):
    lane = lane_id(8)
    out = list(pieces)
    for m in range(3):
        a, b, c = (pltpu.roll(pieces[3 * m + k], 32 + 32 * k, 1) for k in range(3))
        out.append(jnp.where(lane < 32, a, jnp.where(lane < 64, b, c)))
    return out


def column_matrix(centre, after, before):
    row = lax.broadcasted_iota(jnp.int32, (2 * LANES, LANES), 0)
    lane = lax.broadcasted_iota(jnp.int32, (2 * LANES, LANES), 1)
    row = jnp.where(row >= LANES, row - LANES, row)
    gap = row - lane
    weight = jnp.where(
        gap == 0, centre,
        jnp.where(
            (gap == 1) | (gap == 1 - NVX), after,
            jnp.where((gap == -1) | (gap == NVX - 1), before, 0.0),
        ),
    )
    return jnp.where((row < NVX) & (lane < NVX), weight, 0.0).astype(jnp.bfloat16)


def spread_rows(pieces):
    p = [x + y for x, y in zip(pieces, ring_next(pieces))]
    return [x + y for x, y in zip(p, ring_prev(p))]


def split(v):
    high = v.astype(jnp.bfloat16)
    low = (v - high.astype(jnp.float32)).astype(jnp.bfloat16)
    return jnp.concatenate([high, low], axis=1)


def columns(v, matrix):
    return jnp.dot(split(v), matrix, preferred_element_type=jnp.float32)


def tree(values):
    while len(values) > 1:
        pairs = [x + y for x, y in zip(values[::2], values[1::2])]
        values = pairs + values[2 * len(pairs) :]
    return values[0]


def inner(a, b):
    total = a[0] * b[0]
    for x, y in zip(a[1:], b[1:]):
        total = total + x * y
    return total


def combine(moments, shift):
    one = jnp.ones_like(moments[0])
    res_c, dir_c, out = [one], [one], []
    res_m, dir_m = list(moments), list(moments)
    norm = moments[0]
    for turn in range(ITERS):
        image_m = [shift * x + y for x, y in zip(dir_m, dir_m[1:])]
        alpha = norm / inner(dir_c, image_m)
        grown = out + [jnp.zeros_like(one)]
        out = [x + alpha * y for x, y in zip(grown, dir_c)]
        if turn == ITERS - 1:
            return out
        image_c = [shift * dir_c[0]]
        image_c += [shift * x + y for x, y in zip(dir_c[1:], dir_c)] + [dir_c[-1]]
        res_c = [x - alpha * y for x, y in zip(res_c, image_c)] + [-alpha * image_c[-1]]
        res_m = [x - alpha * y for x, y in zip(res_m, image_m)]
        norm_next = inner(res_c, res_m)
        beta = norm_next / norm
        norm = norm_next
        dir_c = [x + beta * y for x, y in zip(res_c, dir_c)] + [res_c[-1]]
        dir_m = [x + beta * y for x, y in zip(res_m, dir_m)]


def rve_kernel(
    depth, groups, slabs, in_dev, volume,
    sub_in, pg_in, pb_in, own_in, p_in, h_in, b_in, d_in, g_in, k_in, y_in,
    v0, v1, v2, v3, v4, w_ref, inbox_ref, elem_ref,
    sub_ref, pg_ref, pb_ref, own_ref,
    p_ref, h_ref, b_ref, d_ref, g_ref, k_ref, y_ref,
    st_ref, acc_ref, hist_ref, tmp_ref, pick_ref,
    sh, c8, ee, ps, red, ms, mr, ab, es, eo, th, tr, tt, td, sp, sr, pk, rk,
    insem, smallsem,
    nsend, nrecv, rsend, rrecv, bsend, brecv, esend, erecv,
):
    group = lax.axis_index("rve")
    slab = lax.axis_index("slab")
    up = lax.rem(slab + 1, slabs)
    down = lax.rem(slab + slabs - 1, slabs)
    last = depth - 1
    vv = (v0, v1, v2, v3, v4)
    ins = (p_ref, h_ref, b_ref, d_ref, g_ref, k_ref, y_ref)
    sources = (p_in, h_in, b_in, d_in, g_in, k_in, y_in)

    early = max(min(4, depth), 2 * (5 * depth // 12))

    chunks = [(0, 0, 1), (0, last, 1), (2, 1, early // 2 - 1), (2, depth - early // 2, early // 2 - 1)]
    chunks.append((early, early // 2, depth - early))
    if depth % 2:
        chunks = [(i, i // 2 if i % 2 == 0 else last - i // 2, 1) for i in range(depth)]
    chunks = [chunk for chunk in chunks if chunk[2] > 0]

    def fetch(n, k):
        at = pl.ds(chunks[n][1], chunks[n][2])
        wide = len(ins[k].shape) == 4
        return pltpu.make_async_copy(
            sources[k].at[:, at] if wide else sources[k].at[at],
            ins[k].at[:, at] if wide else ins[k].at[at],
            insem.at[n, k],
        )

    small = [
        pltpu.make_async_copy(src, dst, smallsem.at[i])
        for i, (src, dst) in enumerate(
            ((sub_in, sub_ref), (pg_in, pg_ref), (pb_in, pb_ref), (own_in, own_ref))
        )
    ]
    small[0].start()
    for n in range(len(chunks)):
        for k in range(7):
            fetch(n, k).start()
    for copy in small[1:]:
        copy.start()
    barrier = pltpu.get_barrier_semaphore()
    for k in range(1, slabs):
        pl.semaphore_signal(
            barrier, inc=1, device_id={"slab": lax.rem(slab + k, slabs)}, device_id_type=MESH
        )
    for k in range(1, groups):
        pl.semaphore_signal(
            barrier, inc=1, device_id={"rve": lax.rem(group + k, groups)}, device_id_type=MESH
        )

    def remote(src, dst, ssem, rsem, axis, to):
        return pltpu.make_async_remote_copy(
            src_ref=src, dst_ref=dst, send_sem=ssem, recv_sem=rsem,
            device_id={axis: to}, device_id_type=MESH,
        )

    def to_slabs(src, dst, ssem, rsem):
        copies = []
        for k in range(1, slabs):
            to = lax.rem(slab + k, slabs)
            copies.append(remote(src, dst.at[slab], ssem.at[k], rsem.at[k], "slab", to))
        return copies

    acc_ref[...] = jnp.zeros_like(acc_ref)
    tt[...] = column_matrix(2.0, 1.0, 1.0)
    td[...] = column_matrix(0.0, 1.0, -1.0)
    small[0].wait()

    def stress_copies(part):
        at = (slice(0, 3), slice(3, 4))[part]
        return [
            remote(
                sp.at[side, at], sr.at[side, at],
                nsend.at[0, part, side], nrecv.at[0, part, side], "slab", to,
            )
            for side, to in enumerate((up, down))
        ]

    def pack_stress():
        for side, z in enumerate((last, 0)):
            for n, f in enumerate((2, 3, 4, 6)):
                for i, v in enumerate(fold(cut(st_ref[f, z]))):
                    sp[side, n, 8 * i : 8 * i + 8] = v

    def unpack_stress():
        for side in range(2):
            for n in range(3):
                for i, v in enumerate(unfold(cut(sr[side, n]))):
                    sh[side, n, 8 * i : 8 * i + 8] = v

    def unpack_coefficient():
        for side, z in enumerate((0, depth + 1)):
            for i, v in enumerate(unfold(cut(sr[side, 3]))):
                c8[z, 8 * i : 8 * i + 8] = 0.125 * v

    def ydiff(v):
        v = cut(v)
        both = [x - y for x, y in zip(ring_next(v), ring_prev(v))]
        return jnp.concatenate(both, axis=0)

    def rhs_plane(z, below, above):
        s3, s4, s5 = st_ref[3, z], st_ref[4, z], st_ref[5, z]
        zd = {c: above(c) - below(c) for c in (2, 3, 4)}
        hr = 0.5 * half_root
        xd = columns(jnp.concatenate([st_ref[0, z], s5, s4], axis=0), td[...])
        f0 = 0.5 * xd[0:NVX] + hr * (ydiff(s5) + zd[4])
        f1 = hr * (xd[NVX : 2 * NVX] + zd[3]) + 0.5 * ydiff(st_ref[1, z])
        f2 = hr * (xd[2 * NVX :] + ydiff(s3)) + 0.5 * zd[2]
        for c, v in enumerate((f0, f1, f2)):
            v0[c, z + 1] = v

    def field_copies(j, c):
        return [
            remote(
                pk.at[j, c, side], rk.at[j, c, side],
                nsend.at[1 + j, c, side], nrecv.at[1 + j, c, side], "slab", to,
            )
            for side, to in enumerate((up, down) if j + 1 < ITERS else (up,))
        ]

    def pack_edges(j, c):
        for side, z in enumerate((depth, 1) if j + 1 < ITERS else (depth,)):
            for i, v in enumerate(fold(cut(vv[j][c, z]))):
                pk[j, c, side, 8 * i : 8 * i + 8] = v

    def unpack_halos(j, c):
        if j + 1 == ITERS:
            for i, v in enumerate(unfold(cut(rk[j, c, 0]))):
                vv[j][c, 0, 8 * i : 8 * i + 8] = v + v
            vv[j][c, depth + 1] = jnp.zeros((NVX, LANES), jnp.float32)
            return
        for side, z in enumerate((0, depth + 1)):
            for i, v in enumerate(unfold(cut(rk[j, c, side]))):
                vv[j][c, z, 8 * i : 8 * i + 8] = v

    def start(copies):
        for copy in copies:
            copy.start()

    def finish(copies):
        for copy in copies:
            copy.wait()

    def material(i):
        z = i // 2 + (i % 2) * (last - 2 * (i // 2))
        base = (slab * depth + z) * 4
        counts = [sub_ref[group, base + q] for q in range(4)]
        material_plane(z, counts, ins, st_ref, acc_ref, hist_ref, tmp_ref)
        c8[z + 1] = st_ref[6, z] * 0.125

    def material_step(turn, _):
        for first in sorted({chunk[0] for chunk in chunks}):

            @pl.when(turn == first)
            def _():
                for n, chunk in enumerate(chunks):
                    if chunk[0] == first:
                        finish([fetch(n, k) for k in range(7)])

        material(turn)

        @pl.when(turn == 1)
        def _():
            pl.semaphore_wait(barrier, slabs + groups - 2)
            pack_stress()
            start(stress_copies(0))
            start(stress_copies(1))

        @pl.when(turn == early - 1)
        def _():
            th[...] = acc_ref[2]
            start(to_slabs(th, tr, rsend.at[2], rrecv.at[2]))
            finish(stress_copies(0))
            unpack_stress()
            rhs_plane(0, lambda c: sh[0, c - 2], lambda c: st_ref[c, 1])
            rhs_plane(last, lambda c: st_ref[c, last - 1], lambda c: sh[1, c - 2])
            for c in range(3):
                pack_edges(0, c)
                start(field_copies(0, c))

        return 0

    lax.fori_loop(0, depth, material_step, 0)
    eo[...] = jnp.broadcast_to(summary_row(acc_ref, volume), (8, LANES))
    means = to_slabs(eo, mr, rsend.at[0], rrecv.at[0])
    start(means)
    mr[slab] = eo[...]
    for copy in small[1:]:
        copy.wait()
    quarter_rows = BLK // LANES
    for g in range(groups):
        chosen = slab * (4 * depth)
        for j in range(in_dev):
            slot = slab * in_dev + j
            chosen = jnp.where(pg_ref[g, slot] == group, pb_ref[g, slot], chosen)
        chosen = jnp.clip(chosen - slab * (4 * depth), 0, 4 * depth - 1)
        z = chosen // 4
        quarter = chosen - 4 * z
        for c in range(7):
            plane = hist_ref[c, z]
            got = plane[0:quarter_rows]
            for q in range(1, 4):
                got = jnp.where(quarter == q, plane[q * quarter_rows : (q + 1) * quarter_rows], got)
            pick_ref[g, c] = got
    moves = []
    for k in range(1, groups):
        to = lax.rem(group + k, groups)
        move = remote(pick_ref.at[to], ab.at[group], bsend.at[k], brecv.at[k], "rve", to)
        move.start()
        moves.append(move)
    ab[group] = pick_ref[group]

    def rhs_inner(z, _):
        rhs_plane(z, lambda c: st_ref[c, z - 1], lambda c: st_ref[c, z + 1])
        return 0

    lax.fori_loop(1, last, rhs_inner, 0, unroll=2)
    finish(stress_copies(1))
    unpack_coefficient()
    tr[slab] = th[...]
    finish(to_slabs(th, tr, rsend.at[2], rrecv.at[2]))
    total = tr[0]
    for k in range(1, slabs):
        total = total + tr[k]
    shift = (SHIFT / (early * slabs * PLANE)) * jnp.sum(total, axis=(0, 1), keepdims=True)

    def diagonal(z, _):
        wide = spread_rows(cut(c8[z - 1] + 2.0 * c8[z] + c8[z + 1]))
        wide = cut(columns(jnp.concatenate(wide, axis=0), tt[...]))
        for i, w in enumerate(wide):
            at = slice(8 * i, 8 * i + 8)
            ee[z, at] = (8.0 * (8.0 + mass_weight) * c8[z, at] - shift) + w
        return 0

    lax.fori_loop(1, depth + 1, diagonal, 0, unroll=3)

    zero = jnp.zeros((8, LANES), jnp.float32)

    def apply_plane(j, c, z, carry):
        norm, curve = carry
        plain, mixed, norms, curves = [], [], [], []
        for i in range(0, NVX, 8):
            at = slice(i, i + 8)
            ra, rb, rc = vv[j][c, z - 1, at], vv[j][c, z, at], vv[j][c, z + 1, at]
            crb = c8[z, at] * rb
            plain.append((ra + rc) + (rb + rb))
            mixed.append((c8[z - 1, at] * ra + c8[z + 1, at] * rc) + (crb + crb))
        both = jnp.concatenate(spread_rows(plain) + spread_rows(mixed), axis=0)
        both = columns(both, tt[...])
        plain, mixed = cut(both[0:NVX]), cut(both[NVX:])
        for i in range(0, NVX, 8):
            at = slice(i, i + 8)
            rb = vv[j][c, z, at]
            image = ee[z, at] * rb - c8[z, at] * plain[i // 8] - mixed[i // 8]
            if j + 1 < ITERS:
                vv[j + 1][c, z, at] = image
            norms.append(rb * rb)
            curves.append(rb * image)
        return norm + tree(norms), curve + tree(curves)

    half = (depth + 1) // 2
    for j in range(ITERS):

        def component(c, carry):
            finish(field_copies(j, c))
            unpack_halos(j, c)
            for z in [1, depth, *range(2, half + 1)]:
                carry = apply_plane(j, c, z, carry)
            if j + 1 < ITERS:
                pack_edges(j + 1, c)
                start(field_copies(j + 1, c))
            for z in range(half + 1, depth):
                carry = apply_plane(j, c, z, carry)
            return carry

        carry = lax.fori_loop(0, 3, component, (zero, zero))
        if j == 1:
            finish(means)
            total = mr[0]
            for k in range(1, slabs):
                total = total + mr[k]
            ms[...] = total
            element = [
                remote(ms, es.at[group], esend.at[k], erecv.at[k], "rve", lax.rem(group + k, groups))
                for k in range(1, groups)
            ]
            start(element)
            es[group] = total
        ps[2 * j : 2 * j + 1] = jnp.sum(carry[0], axis=0, keepdims=True)
        ps[2 * j + 1 : 2 * j + 2] = jnp.sum(carry[1], axis=0, keepdims=True)
    ps[2 * ITERS :] = jnp.zeros((ps.shape[0] - 2 * ITERS, LANES), jnp.float32)

    copies = to_slabs(ps, red, rsend.at[1], rrecv.at[1])
    start(copies)
    red[slab] = ps[...]
    for move in moves:
        move.wait()
    for j in range(in_dev):
        source = pg_ref[group, slab * in_dev + j]
        got = ab[jnp.clip(source, 0, groups - 1)]
        for c in range(7):
            inbox_ref[c, :, j, :] = got[c]
    for copy in element:
        copy.wait()
    mine = jnp.zeros((1, LANES), jnp.float32)
    for k in range(groups):
        mine = mine + jnp.where(own_ref[k] == group, es[k][0:1], 0.0)
    elem_ref[...] = mine[:, 0:42]

    for copy in copies:
        copy.wait()
    moments = red[0]
    for k in range(1, slabs):
        moments = moments + red[k]
    moments = jnp.where(lane_id(ps.shape[0]) < NVX, moments, 0.0)
    moments = jnp.sum(moments, axis=1, keepdims=True)
    weights = combine([moments[k : k + 1] for k in range(2 * ITERS)], shift)
    for j, w in enumerate(weights):
        w_ref[j] = jnp.broadcast_to(w, (8, LANES))


def result_kernel(
    depth, v0, v1, v2, v3, v4, w_ref, inbox_ref, elem_ref,
    out_hbm, inbox_hbm, elem_hbm, out_ref, sems, othersems,
):
    others = [
        pltpu.make_async_copy(inbox_ref, inbox_hbm, othersems.at[0]),
        pltpu.make_async_copy(elem_ref, elem_hbm, othersems.at[1]),
    ]
    for copy in others:
        copy.start()
    weights = [w_ref[j] for j in range(ITERS)]

    def leave(z):
        return pltpu.make_async_copy(out_ref.at[:, z], out_hbm.at[:, z], sems.at[z])

    def to_flat(z, _):
        for c in range(3):
            for g in range(NVX // 32):
                rows4 = []
                for r in range(4):
                    at = slice(8 * (4 * g + r), 8 * (4 * g + r) + 8)
                    rows4.append(inner(weights, [v[c, z + 1, at] for v in (v0, v1, v2, v3, v4)]))
                for t, v in enumerate(pack_rows(rows4)):
                    out_ref[c, z, pl.ds(3 * g + t, 8, stride=9)] = v
        leave(z).start()
        return 0

    lax.fori_loop(0, depth, to_flat, 0, unroll=2)

    def left(z, _):
        leave(z).wait()
        return 0

    lax.fori_loop(0, depth, left, 0)
    for copy in others:
        copy.wait()


def on_device(
    groups, slabs,
    plastic_strain, hardening_var, strain_start, strain_step, shear_mod, bulk_mod, yield_stress,
    substeps, pull_group, pull_block, owner,
):
    depth = plastic_strain.shape[2]
    in_dev = pull_group.shape[1] // slabs
    volume = float(depth * slabs * PLANE)
    vmem = pl.BlockSpec(memory_space=pltpu.VMEM)
    hbm = pl.BlockSpec(memory_space=pl.ANY)
    f32 = jnp.float32
    tiles = PLANE // LANES

    def stay(x):
        return pltpu.with_memory_space_constraint(x, pltpu.HBM)

    def view6(x):
        return stay(x.reshape(6, depth, tiles, LANES))

    def view1(x):
        return stay(x.reshape(depth, tiles, LANES))

    pick_shape = (groups, 7, BLK // LANES, LANES)
    plane = (NVX, LANES)
    flat = (tiles, LANES)
    dma = pltpu.SemaphoreType.DMA
    ints = [pltpu.SMEM(x.shape, jnp.int32) for x in (substeps, pull_group, pull_block, owner)]
    six, one = pltpu.VMEM((6, depth) + flat, f32), pltpu.VMEM((depth,) + flat, f32)
    field = jax.ShapeDtypeStruct((3, depth + 2) + plane, f32)
    *fields, weights, inbox, element_sums = pl.pallas_call(
        functools.partial(rve_kernel, depth, groups, slabs, in_dev, volume),
        in_specs=[hbm] * 11,
        out_specs=[vmem] * 8,
        out_shape=[
            *[field] * ITERS,
            jax.ShapeDtypeStruct((ITERS, 8, LANES), f32),
            jax.ShapeDtypeStruct((7, BLK // LANES, in_dev, LANES), f32),
            jax.ShapeDtypeStruct((1, 42), f32),
        ],
        scratch_shapes=[
            *ints,
            six, one, six, six, one, one, one,
            pltpu.VMEM((7, depth) + plane, f32),
            pltpu.VMEM((8 + len(PAIRS), 8, LANES), f32),
            pltpu.VMEM((7, depth) + flat, f32),
            pltpu.VMEM((7,) + flat, f32),
            pltpu.VMEM(pick_shape, f32),
            pltpu.VMEM((2, 3) + plane, f32),
            pltpu.VMEM((depth + 2,) + plane, f32),
            pltpu.VMEM((depth + 2,) + plane, f32),
            pltpu.VMEM((16, LANES), f32),
            pltpu.VMEM((slabs, 16, LANES), f32),
            pltpu.VMEM((8, LANES), f32),
            pltpu.VMEM((slabs, 8, LANES), f32),
            pltpu.VMEM(pick_shape, f32),
            pltpu.VMEM((groups, 8, LANES), f32),
            pltpu.VMEM((8, LANES), f32),
            pltpu.VMEM((8, LANES), f32),
            pltpu.VMEM((slabs, 8, LANES), f32),
            pltpu.VMEM((2 * LANES, LANES), jnp.bfloat16),
            pltpu.VMEM((2 * LANES, LANES), jnp.bfloat16),
            pltpu.VMEM((2, 4) + flat, f32),
            pltpu.VMEM((2, 4) + flat, f32),
            pltpu.VMEM((ITERS, 3, 2) + flat, f32),
            pltpu.VMEM((ITERS, 3, 2) + flat, f32),
            dma((max(depth, 5), 7)),
            dma((4,)),
            dma((ITERS + 1, 3, 2)),
            dma((ITERS + 1, 3, 2)),
            dma((3, slabs)),
            dma((3, slabs)),
            dma((groups,)),
            dma((groups,)),
            dma((groups,)),
            dma((groups,)),
        ],
        compiler_params=pltpu.CompilerParams(
            collective_id=0, has_side_effects=True, vmem_limit_bytes=32 * 1024 * 1024
        ),
        name="rve_step",
    )(
        stay(substeps), stay(pull_group), stay(pull_block), stay(owner),
        view6(plastic_strain), view1(hardening_var), view6(strain_start), view6(strain_step),
        view1(shear_mod), view1(bulk_mod), view1(yield_stress),
    )
    correction, inbox, element_sums = pl.pallas_call(
        functools.partial(result_kernel, depth),
        in_specs=[vmem] * 8,
        out_specs=[hbm] * 3,
        out_shape=[
            jax.ShapeDtypeStruct((3, depth, tiles, LANES), f32),
            jax.ShapeDtypeStruct((7, BLK // LANES, in_dev, LANES), f32),
            jax.ShapeDtypeStruct((1, 42), f32),
        ],
        scratch_shapes=[pltpu.VMEM((3, depth) + flat, f32), dma((depth,)), dma((2,))],
        compiler_params=pltpu.CompilerParams(vmem_limit_bytes=8 * 1024 * 1024),
        name="result",
    )(*fields, weights, inbox, element_sums)
    correction = correction.reshape(3, 1, depth, PLANE)
    inbox = inbox.swapaxes(1, 2).reshape(7, 1, in_dev, BLK)
    return correction, inbox, element_sums


def solution(mesh):
    return jax.shard_map(
        functools.partial(on_device, mesh.shape["rve"], mesh.shape["slab"]),
        mesh=mesh,
        in_specs=(
            P(None, "rve", "slab", None),
            P("rve", "slab", None),
            P(None, "rve", "slab", None),
            P(None, "rve", "slab", None),
            P("rve", "slab", None),
            P("rve", "slab", None),
            P("rve", "slab", None),
            P(),
            P(),
            P(),
            P(),
        ),
        out_specs=(P(None, "rve", "slab", None), P(None, "rve", "slab", None), P("rve", None)),
        check_vma=False,
    )
```

```python
import functools
import math

import jax
import jax.numpy as jnp
from jax import lax
from jax.experimental import pallas as pl
from jax.experimental.pallas import tpu as pltpu
from jax.sharding import PartitionSpec as P

NVX = 96
ITERS = 5
SUBMAX = 8
PLANE = 9216
BLK = 2304
LANES = 128
PART = 24
MEAN_LANE = 42
SHIFT = 12.0
MESH = pl.DeviceIdType.MESH

hard_ratio = 0.3
mass_weight = 0.05
root_two_thirds = math.sqrt(2.0 / 3.0)
half_root = 1.0 / math.sqrt(2.0)
KEPT = (0, 1, 3, 4, 5)
PAIRS = tuple((i, j) for i in range(5) for j in range(i, 5))


def lane_id(rows):
    return lax.broadcasted_iota(jnp.int32, (rows, LANES), 1)


def unpack_rows(a, b, c):
    lane = lane_id(a.shape[0])
    plain = (
        a,
        pltpu.roll(jnp.where(lane >= 96, a, b), 32, 1),
        pltpu.roll(jnp.where(lane >= 64, b, c), 64, 1),
        pltpu.roll(c, 96, 1),
    )
    return plain


def pack_rows(rows4):
    t0, t1, t2, t3 = rows4
    lane = lane_id(t0.shape[0])
    r1, r2, r3 = pltpu.roll(t1, 96, 1), pltpu.roll(t2, 64, 1), pltpu.roll(t3, 32, 1)
    return (
        jnp.where(lane < 96, t0, r1),
        jnp.where(lane < 64, r1, r2),
        jnp.where(lane < 32, r2, r3),
    )


def norm_form(a, b):
    return (
        a[0] * (b[0] + b[0] + b[1]) + a[1] * (b[0] + b[1] + b[1])
        + a[2] * b[2] + a[3] * b[3] + a[4] * b[4]
    )


def deviator(vals):
    trace = vals[0] + vals[1] + vals[2]
    third = trace * (1.0 / 3.0)
    return [vals[0] - third, vals[1] - third, vals[3], vals[4], vals[5]], trace


def full(five):
    return [five[0], five[1], -(five[0] + five[1]), five[2], five[3], five[4]]


def material_plane(z, counts, ins, st_ref, acc_ref, hist_ref, tmp_ref):
    p_ref, h_ref, b_ref, d_ref, g_ref, k_ref, y_ref = ins
    tiles = PLANE // LANES
    parts = tuple(slice(t, t + PART) for t in range(0, tiles, PART))
    quarter_rows = BLK // LANES

    def strains(rows):
        dev0, tr0 = deviator([b_ref[c, z, rows] - p_ref[c, z, rows] for c in range(6)])
        devs, trs = deviator([d_ref[c, z, rows] for c in range(6)])
        return dev0, devs, tr0 + trs

    state = []
    for rows in parts:
        row = lax.broadcasted_iota(jnp.int32, (PART, LANES), 0) + rows.start
        count = jnp.full((PART, LANES), counts[0], jnp.int32)
        for q in range(1, 4):
            count = jnp.where(row >= q * quarter_rows, counts[q], count)
        count = count.astype(jnp.float32)
        inv = 1.0 / count
        dev0, devs, _ = strains(rows)
        s00 = norm_form(dev0, dev0)
        s01 = 2.0 * inv * norm_form(dev0, devs)
        s11 = inv * inv * norm_form(devs, devs)
        level = (11.0 * root_two_thirds / 2.2) * (
            y_ref[z, rows] / g_ref[z, rows] + hard_ratio * h_ref[z, rows]
        )
        state.append([jnp.ones_like(inv), count - float(SUBMAX), level, level, s00, s01, s11, inv])
    for turn in range(SUBMAX - 1):
        for one in state:
            a, b, level, _, s00, s01, s11, _ = one
            b = b + 1.0
            square = jnp.maximum(a * (a * s00 + b * s01) + (b * b) * s11, 1e-30)
            rs = lax.rsqrt(square)
            fac = jnp.minimum((1.0 + level * rs) * (1.0 / 11.0), 1.0)
            fac = jnp.where(b > 0.0, fac, 1.0)
            one[2] = level + (1.0 - fac) * (square * rs)
            one[0] = a * fac
            one[1] = b * fac
    sums = [None] * (8 + len(PAIRS))
    for rows, one in zip(parts, state):
        a, b, level, level0, _, _, _, inv = one
        b = (b + 1.0) * inv
        dev0, devs, trace = strains(rows)
        dd = [a * x + b * y for x, y in zip(dev0, devs)]
        square = jnp.maximum(norm_form(dd, dd), 1e-30)
        rs = lax.rsqrt(square)
        fac = jnp.minimum((1.0 + level * rs) * (1.0 / 11.0), 1.0)
        level = level + (1.0 - fac) * (square * rs)
        fin = [fac * v for v in dd]
        mu = g_ref[z, rows]
        coef = mu * fac
        weight = (coef - mu) * (rs * rs)
        bulk = k_ref[z, rows]
        vol = bulk * trace
        two_mu = 2.0 * mu
        ms = [two_mu * v for v in fin]
        wn = [weight * v for v in dd]
        gone = full([x + y - w for x, y, w in zip(dev0, devs, fin)])
        for c, v in enumerate(full(ms)):
            tmp_ref[c, rows] = v + vol if c < 3 else v
            hist_ref[c, z, rows] = p_ref[c, z, rows] + gone[c]
        tmp_ref[6, rows] = coef
        hist_ref[6, z, rows] = h_ref[z, rows] + root_two_thirds * (level - level0)
        terms = [vol, bulk, coef] + ms + [wn[i] * dd[j] for i, j in PAIRS]
        for t, v in enumerate(terms):
            for o in range(0, PART, 8):
                piece = v[o : o + 8]
                sums[t] = piece if sums[t] is None else sums[t] + piece
    for t, v in enumerate(sums):
        acc_ref[t] += v
    for f in range(7):
        for g in range(tiles // 24):
            a, b, c = (tmp_ref[f, pl.ds(3 * g + k, 8, stride=9)] for k in range(3))
            for r, rowv in enumerate(unpack_rows(a, b, c)):
                at = 8 * (4 * g + r)
                st_ref[f, z, at : at + 8] = rowv


def summary_row(acc_ref, volume):
    tot = [
        jnp.sum(acc_ref[t], axis=(0, 1), keepdims=True) * (1.0 / volume)
        for t in range(8 + len(PAIRS))
    ]
    vol, bulk, coef = tot[0], tot[1], tot[2]
    ms = tot[3:8]
    stress = [vol + ms[0], vol + ms[1], vol - ms[0] - ms[1], ms[2], ms[3], ms[4]]
    table = {}
    for t, (i, j) in enumerate(PAIRS):
        table[(KEPT[i], KEPT[j])] = tot[8 + t]
        table[(KEPT[j], KEPT[i])] = tot[8 + t]
    for j in KEPT:
        table[(2, j)] = -(table[(0, j)] + table[(1, j)])
        table[(j, 2)] = table[(2, j)]
    table[(2, 2)] = -(table[(2, 0)] + table[(2, 1)])
    lane = lane_id(1)
    row = jnp.zeros((1, LANES), jnp.float32)
    for c in range(6):
        row = jnp.where(lane == c, stress[c], row)
    for i in range(6):
        for j in range(6):
            v = 2.0 * table[(i, j)]
            if i == j:
                v = v + 2.0 * coef
            if i < 3 and j < 3:
                v = v + bulk - (2.0 / 3.0) * coef
            row = jnp.where(lane == 6 + 6 * i + j, v, row)
    return jnp.where(lane == MEAN_LANE, coef, row)


def ring_next(pieces):
    return pieces[1:] + [pltpu.roll(pieces[0], 7, 0)]


def ring_prev(pieces):
    return [pltpu.roll(pieces[-1], 1, 0)] + pieces[:-1]


def cut(v):
    return [v[i : i + 8] for i in range(0, v.shape[0], 8)]


def fold(pieces):
    lane = lane_id(8)
    return [
        jnp.where(lane < NVX, pieces[i], pltpu.roll(pieces[9 + i // 3], 96 - 32 * (i % 3), 1))
        for i in range(9)
    ]


def unfold(pieces):
    lane = lane_id(8)
    out = list(pieces)
    for m in range(3):
        a, b, c = (pltpu.roll(pieces[3 * m + k], 32 + 32 * k, 1) for k in range(3))
        out.append(jnp.where(lane < 32, a, jnp.where(lane < 64, b, c)))
    return out


def column_matrix(centre, after, before):
    row = lax.broadcasted_iota(jnp.int32, (2 * LANES, LANES), 0)
    lane = lax.broadcasted_iota(jnp.int32, (2 * LANES, LANES), 1)
    row = jnp.where(row >= LANES, row - LANES, row)
    gap = row - lane
    weight = jnp.where(
        gap == 0, centre,
        jnp.where(
            (gap == 1) | (gap == 1 - NVX), after,
            jnp.where((gap == -1) | (gap == NVX - 1), before, 0.0),
        ),
    )
    return jnp.where((row < NVX) & (lane < NVX), weight, 0.0).astype(jnp.bfloat16)


def spread_rows(pieces):
    p = [x + y for x, y in zip(pieces, ring_next(pieces))]
    return [x + y for x, y in zip(p, ring_prev(p))]


def split(v):
    high = v.astype(jnp.bfloat16)
    low = (v - high.astype(jnp.float32)).astype(jnp.bfloat16)
    return jnp.concatenate([high, low], axis=1)


def columns(v, matrix):
    return jnp.dot(split(v), matrix, preferred_element_type=jnp.float32)


def tree(values):
    while len(values) > 1:
        pairs = [x + y for x, y in zip(values[::2], values[1::2])]
        values = pairs + values[2 * len(pairs) :]
    return values[0]


def inner(a, b):
    total = a[0] * b[0]
    for x, y in zip(a[1:], b[1:]):
        total = total + x * y
    return total


def combine(moments, shift):
    one = jnp.ones_like(moments[0])
    res_c, dir_c, out = [one], [one], []
    res_m, dir_m = list(moments), list(moments)
    norm = moments[0]
    for turn in range(ITERS):
        image_m = [shift * x + y for x, y in zip(dir_m, dir_m[1:])]
        alpha = norm / inner(dir_c, image_m)
        grown = out + [jnp.zeros_like(one)]
        out = [x + alpha * y for x, y in zip(grown, dir_c)]
        if turn == ITERS - 1:
            return out
        image_c = [shift * dir_c[0]]
        image_c += [shift * x + y for x, y in zip(dir_c[1:], dir_c)] + [dir_c[-1]]
        res_c = [x - alpha * y for x, y in zip(res_c, image_c)] + [-alpha * image_c[-1]]
        res_m = [x - alpha * y for x, y in zip(res_m, image_m)]
        norm_next = inner(res_c, res_m)
        beta = norm_next / norm
        norm = norm_next
        dir_c = [x + beta * y for x, y in zip(res_c, dir_c)] + [res_c[-1]]
        dir_m = [x + beta * y for x, y in zip(res_m, dir_m)]


def rve_kernel(
    depth, groups, slabs, in_dev, volume,
    sub_in, pg_in, pb_in, own_in, p_in, h_in, b_in, d_in, g_in, k_in, y_in,
    v0, v1, v2, v3, v4, w_ref, inbox_ref, elem_ref,
    sub_ref, pg_ref, pb_ref, own_ref,
    p_ref, h_ref, b_ref, d_ref, g_ref, k_ref, y_ref,
    st_ref, acc_ref, hist_ref, tmp_ref, pick_ref,
    sh, c8, ee, ps, red, ms, mr, ab, es, eo, th, tr, tt, td, sp, sr, pk, rk,
    insem, smallsem,
    nsend, nrecv, rsend, rrecv, bsend, brecv, esend, erecv,
):
    group = lax.axis_index("rve")
    slab = lax.axis_index("slab")
    up = lax.rem(slab + 1, slabs)
    down = lax.rem(slab + slabs - 1, slabs)
    last = depth - 1
    vv = (v0, v1, v2, v3, v4)
    ins = (p_ref, h_ref, b_ref, d_ref, g_ref, k_ref, y_ref)
    sources = (p_in, h_in, b_in, d_in, g_in, k_in, y_in)

    early = max(min(4, depth), 2 * (5 * depth // 12))

    chunks = [(0, 0, 1), (0, last, 1), (2, 1, early // 2 - 1), (2, depth - early // 2, early // 2 - 1)]
    chunks.append((early, early // 2, depth - early))
    if depth % 2:
        chunks = [(i, i // 2 if i % 2 == 0 else last - i // 2, 1) for i in range(depth)]
    chunks = [chunk for chunk in chunks if chunk[2] > 0]

    def fetch(n, k):
        at = pl.ds(chunks[n][1], chunks[n][2])
        wide = len(ins[k].shape) == 4
        return pltpu.make_async_copy(
            sources[k].at[:, at] if wide else sources[k].at[at],
            ins[k].at[:, at] if wide else ins[k].at[at],
            insem.at[n, k],
        )

    small = [
        pltpu.make_async_copy(src, dst, smallsem.at[i])
        for i, (src, dst) in enumerate(
            ((sub_in, sub_ref), (pg_in, pg_ref), (pb_in, pb_ref), (own_in, own_ref))
        )
    ]
    small[0].start()
    for n in range(len(chunks)):
        for k in range(7):
            fetch(n, k).start()
    for copy in small[1:]:
        copy.start()
    barrier = pltpu.get_barrier_semaphore()
    for k in range(1, slabs):
        pl.semaphore_signal(
            barrier, inc=1, device_id={"slab": lax.rem(slab + k, slabs)}, device_id_type=MESH
        )
    for k in range(1, groups):
        pl.semaphore_signal(
            barrier, inc=1, device_id={"rve": lax.rem(group + k, groups)}, device_id_type=MESH
        )

    def remote(src, dst, ssem, rsem, axis, to):
        return pltpu.make_async_remote_copy(
            src_ref=src, dst_ref=dst, send_sem=ssem, recv_sem=rsem,
            device_id={axis: to}, device_id_type=MESH,
        )

    def to_slabs(src, dst, ssem, rsem):
        copies = []
        for k in range(1, slabs):
            to = lax.rem(slab + k, slabs)
            copies.append(remote(src, dst.at[slab], ssem.at[k], rsem.at[k], "slab", to))
        return copies

    acc_ref[...] = jnp.zeros_like(acc_ref)
    tt[...] = column_matrix(2.0, 1.0, 1.0)
    td[...] = column_matrix(0.0, 1.0, -1.0)
    small[0].wait()

    def stress_copies(part):
        at = (slice(0, 3), slice(3, 5))[part]
        return [
            remote(
                sp.at[side, at], sr.at[side, at],
                nsend.at[0, part, side], nrecv.at[0, part, side], "slab", to,
            )
            for side, to in enumerate((up, down))
        ]

    def pack_plane(v, into, at):
        for i, piece in enumerate(fold(cut(v))):
            into[(*at, slice(8 * i, 8 * i + 8))] = piece

    def pack_stress():
        for side, z in enumerate((last, 0)):
            for n, f in enumerate((2, 3, 4)):
                pack_plane(st_ref[f, z], sp, (side, n))

    def pack_coefficient():
        for side, zs in enumerate(((last - 1, last), (0, 1))):
            for n, z in enumerate(zs):
                pack_plane(st_ref[6, z], sp, (side, 3 + n))

    def unpack_stress():
        for side in range(2):
            for n in range(3):
                for i, v in enumerate(unfold(cut(sr[side, n]))):
                    sh[side, n, 8 * i : 8 * i + 8] = v

    def unpack_coefficient():
        for side, zs in enumerate(((0, 1), (depth + 2, depth + 3))):
            for n, z in enumerate(zs):
                for i, v in enumerate(unfold(cut(sr[side, 3 + n]))):
                    c8[z, 8 * i : 8 * i + 8] = 0.125 * v

    def ydiff(v):
        v = cut(v)
        both = [x - y for x, y in zip(ring_next(v), ring_prev(v))]
        return jnp.concatenate(both, axis=0)

    def rhs_plane(z, below, above):
        s3, s4, s5 = st_ref[3, z], st_ref[4, z], st_ref[5, z]
        zd = {c: above(c) - below(c) for c in (2, 3, 4)}
        hr = 0.5 * half_root
        xd = columns(jnp.concatenate([st_ref[0, z], s5, s4], axis=0), td[...])
        f0 = 0.5 * xd[0:NVX] + hr * (ydiff(s5) + zd[4])
        f1 = hr * (xd[NVX : 2 * NVX] + zd[3]) + 0.5 * ydiff(st_ref[1, z])
        f2 = hr * (xd[2 * NVX :] + ydiff(s3)) + 0.5 * zd[2]
        for c, v in enumerate((f0, f1, f2)):
            v0[c, z + 2] = v

    def field_copies(j, c):
        if j + 1 == ITERS:
            pairs = [(pk.at[j // 2, c, 0, 1], rk.at[j // 2, c, 0, 1], up)]
        else:
            pairs = [(pk.at[j // 2, c, n], rk.at[j // 2, c, n], to) for n, to in ((0, up), (1, down))]
        return [
            remote(src, dst, nsend.at[1 + j, c, side], nrecv.at[1 + j, c, side], "slab", to)
            for side, (src, dst, to) in enumerate(pairs)
        ]

    def pack_edges(j, c):
        if j + 1 == ITERS:
            pack_plane(vv[j][c, depth + 1], pk, (j // 2, c, 0, 1))
            return
        for side, zs in enumerate(((depth, depth + 1), (2, 3))):
            for n, z in enumerate(zs):
                pack_plane(vv[j][c, z], pk, (j // 2, c, side, n))

    def unpack_halos(j, c):
        if j + 1 == ITERS:
            for i, v in enumerate(unfold(cut(rk[j // 2, c, 0, 1]))):
                vv[j][c, 1, 8 * i : 8 * i + 8] = v + v
            return
        for side, zs in enumerate(((0, 1), (depth + 2, depth + 3))):
            for n, z in enumerate(zs):
                for i, v in enumerate(unfold(cut(rk[j // 2, c, side, n]))):
                    vv[j][c, z, 8 * i : 8 * i + 8] = v

    def start(copies):
        for copy in copies:
            copy.start()

    def finish(copies):
        for copy in copies:
            copy.wait()

    def material(i):
        z = i // 2 + (i % 2) * (last - 2 * (i // 2))
        base = (slab * depth + z) * 4
        counts = [sub_ref[group, base + q] for q in range(4)]
        material_plane(z, counts, ins, st_ref, acc_ref, hist_ref, tmp_ref)
        c8[z + 2] = st_ref[6, z] * 0.125

    def material_step(turn, _):
        for first in sorted({chunk[0] for chunk in chunks}):

            @pl.when(turn == first)
            def _():
                for n, chunk in enumerate(chunks):
                    if chunk[0] == first:
                        finish([fetch(n, k) for k in range(7)])

        material(turn)

        @pl.when(turn == 1)
        def _():
            pl.semaphore_wait(barrier, slabs + groups - 2)
            pack_stress()
            start(stress_copies(0))

        @pl.when(turn == min(3, last))
        def _():
            pack_coefficient()
            start(stress_copies(1))

        @pl.when(turn == early - 1)
        def _():
            th[...] = acc_ref[2]
            start(to_slabs(th, tr, rsend.at[2], rrecv.at[2]))
            finish(stress_copies(0))
            unpack_stress()
            for z in sorted({0, 1, last - 1, last}):
                rhs_plane(
                    z,
                    lambda c, z=z: st_ref[c, z - 1] if z > 0 else sh[0, c - 2],
                    lambda c, z=z: st_ref[c, z + 1] if z < last else sh[1, c - 2],
                )
            for c in range(3):
                pack_edges(0, c)
                start(field_copies(0, c))

        return 0

    lax.fori_loop(0, depth, material_step, 0)
    eo[...] = jnp.broadcast_to(summary_row(acc_ref, volume), (8, LANES))
    means = to_slabs(eo, mr, rsend.at[0], rrecv.at[0])
    start(means)
    mr[slab] = eo[...]
    for copy in small[1:]:
        copy.wait()
    quarter_rows = BLK // LANES
    for g in range(groups):
        chosen = slab * (4 * depth)
        for j in range(in_dev):
            slot = slab * in_dev + j
            chosen = jnp.where(pg_ref[g, slot] == group, pb_ref[g, slot], chosen)
        chosen = jnp.clip(chosen - slab * (4 * depth), 0, 4 * depth - 1)
        z = chosen // 4
        quarter = chosen - 4 * z
        for c in range(7):
            plane = hist_ref[c, z]
            got = plane[0:quarter_rows]
            for q in range(1, 4):
                got = jnp.where(quarter == q, plane[q * quarter_rows : (q + 1) * quarter_rows], got)
            pick_ref[g, c] = got
    moves = []
    for k in range(1, groups):
        to = lax.rem(group + k, groups)
        move = remote(pick_ref.at[to], ab.at[group], bsend.at[k], brecv.at[k], "rve", to)
        move.start()
        moves.append(move)
    ab[group] = pick_ref[group]

    def rhs_inner(z, _):
        rhs_plane(z, lambda c: st_ref[c, z - 1], lambda c: st_ref[c, z + 1])
        return 0

    if last - 1 > 2:
        lax.fori_loop(2, last - 1, rhs_inner, 0, unroll=2)
    finish(stress_copies(1))
    unpack_coefficient()
    tr[slab] = th[...]
    finish(to_slabs(th, tr, rsend.at[2], rrecv.at[2]))
    total = tr[0]
    for k in range(1, slabs):
        total = total + tr[k]
    shift = (SHIFT / (early * slabs * PLANE)) * jnp.sum(total, axis=(0, 1), keepdims=True)

    def diagonal(z, _):
        wide = spread_rows(cut(c8[z - 1] + 2.0 * c8[z] + c8[z + 1]))
        wide = cut(columns(jnp.concatenate(wide, axis=0), tt[...]))
        for i, w in enumerate(wide):
            at = slice(8 * i, 8 * i + 8)
            ee[z, at] = (8.0 * (8.0 + mass_weight) * c8[z, at] - shift) + w
        return 0

    lax.fori_loop(1, depth + 3, diagonal, 0, unroll=2)

    zero = jnp.zeros((8, LANES), jnp.float32)

    def apply_plane(j, c, z, carry):
        norm, curve = carry
        plain, mixed, norms, curves = [], [], [], []
        for i in range(0, NVX, 8):
            at = slice(i, i + 8)
            ra, rb, rc = vv[j][c, z - 1, at], vv[j][c, z, at], vv[j][c, z + 1, at]
            crb = c8[z, at] * rb
            plain.append((ra + rc) + (rb + rb))
            mixed.append((c8[z - 1, at] * ra + c8[z + 1, at] * rc) + (crb + crb))
        both = jnp.concatenate(spread_rows(plain) + spread_rows(mixed), axis=0)
        both = columns(both, tt[...])
        plain, mixed = cut(both[0:NVX]), cut(both[NVX:])
        for i in range(0, NVX, 8):
            at = slice(i, i + 8)
            rb = vv[j][c, z, at]
            image = ee[z, at] * rb - c8[z, at] * plain[i // 8] - mixed[i // 8]
            if j + 1 < ITERS:
                vv[j + 1][c, z, at] = image
            norms.append(rb * rb)
            curves.append(rb * image)
        if z < 2 or z > depth + 1:
            return carry
        return norm + tree(norms), curve + tree(curves)

    own = range(2, depth + 2)
    outer = list(dict.fromkeys((2, depth + 1, 3, depth)))

    def apply_planes(j, c, zs, carry):
        for z in zs:
            carry = apply_plane(j, c, z, carry)
        return carry

    for c in range(3):
        vv[ITERS - 1][c, depth + 2] = jnp.zeros((NVX, LANES), jnp.float32)
    for j in range(ITERS):

        def with_send(c, carry):
            first = outer if j + 2 < ITERS else (depth + 1, depth)
            carry = apply_planes(j, c, first, carry)
            pack_edges(j + 1, c)
            start(field_copies(j + 1, c))
            return apply_planes(j, c, [z for z in own if z not in first], carry)

        def inside(c, carry):
            return apply_planes(j, c, range(3, depth + 1 if j + 1 < ITERS else depth + 2), carry)

        def outside(c, carry):
            finish(field_copies(j, c))
            unpack_halos(j, c)
            return apply_planes(j, c, (1, 2, depth + 1, depth + 2), carry)

        carry = (zero, zero)
        if j % 2:
            carry = lax.fori_loop(0, 3, with_send, carry)
        else:
            carry = lax.fori_loop(0, 3, inside, carry)
            if j + 1 < ITERS:
                carry = lax.fori_loop(0, 3, outside, carry)
            else:
                for c in range(3):
                    finish(field_copies(j, c))
                for c in range(3):
                    unpack_halos(j, c)
                for c in range(3):
                    carry = apply_plane(j, c, 2, carry)
        if j == 1:
            finish(means)
            total = mr[0]
            for k in range(1, slabs):
                total = total + mr[k]
            ms[...] = total
            element = [
                remote(ms, es.at[group], esend.at[k], erecv.at[k], "rve", lax.rem(group + k, groups))
                for k in range(1, groups)
            ]
            start(element)
            es[group] = total
        ps[2 * j : 2 * j + 1] = jnp.sum(carry[0], axis=0, keepdims=True)
        ps[2 * j + 1 : 2 * j + 2] = jnp.sum(carry[1], axis=0, keepdims=True)
    ps[2 * ITERS :] = jnp.zeros((ps.shape[0] - 2 * ITERS, LANES), jnp.float32)

    copies = to_slabs(ps, red, rsend.at[1], rrecv.at[1])
    start(copies)
    red[slab] = ps[...]
    for move in moves:
        move.wait()
    for j in range(in_dev):
        source = pg_ref[group, slab * in_dev + j]
        got = ab[jnp.clip(source, 0, groups - 1)]
        for c in range(7):
            inbox_ref[c, :, j, :] = got[c]
    for copy in element:
        copy.wait()
    mine = jnp.zeros((1, LANES), jnp.float32)
    for k in range(groups):
        mine = mine + jnp.where(own_ref[k] == group, es[k][0:1], 0.0)
    elem_ref[...] = mine[:, 0:42]

    for copy in copies:
        copy.wait()
    moments = red[0]
    for k in range(1, slabs):
        moments = moments + red[k]
    moments = jnp.where(lane_id(ps.shape[0]) < NVX, moments, 0.0)
    moments = jnp.sum(moments, axis=1, keepdims=True)
    weights = combine([moments[k : k + 1] for k in range(2 * ITERS)], shift)
    for j, w in enumerate(weights):
        w_ref[j] = jnp.broadcast_to(w, (8, LANES))


def result_kernel(
    depth, v0, v1, v2, v3, v4, w_ref, inbox_ref, elem_ref,
    out_hbm, inbox_hbm, elem_hbm, out_ref, sems, othersems,
):
    others = [
        pltpu.make_async_copy(inbox_ref, inbox_hbm, othersems.at[0]),
        pltpu.make_async_copy(elem_ref, elem_hbm, othersems.at[1]),
    ]
    for copy in others:
        copy.start()
    weights = [w_ref[j] for j in range(ITERS)]

    def leave(z):
        return pltpu.make_async_copy(out_ref.at[:, z], out_hbm.at[:, z], sems.at[z])

    def to_flat(z, _):
        for c in range(3):
            for g in range(NVX // 32):
                rows4 = []
                for r in range(4):
                    at = slice(8 * (4 * g + r), 8 * (4 * g + r) + 8)
                    rows4.append(inner(weights, [v[c, z + 2, at] for v in (v0, v1, v2, v3, v4)]))
                for t, v in enumerate(pack_rows(rows4)):
                    out_ref[c, z, pl.ds(3 * g + t, 8, stride=9)] = v
        leave(z).start()
        return 0

    lax.fori_loop(0, depth, to_flat, 0, unroll=2)

    def left(z, _):
        leave(z).wait()
        return 0

    lax.fori_loop(0, depth, left, 0)
    for copy in others:
        copy.wait()


def on_device(
    groups, slabs,
    plastic_strain, hardening_var, strain_start, strain_step, shear_mod, bulk_mod, yield_stress,
    substeps, pull_group, pull_block, owner,
):
    depth = plastic_strain.shape[2]
    in_dev = pull_group.shape[1] // slabs
    volume = float(depth * slabs * PLANE)
    vmem = pl.BlockSpec(memory_space=pltpu.VMEM)
    hbm = pl.BlockSpec(memory_space=pl.ANY)
    f32 = jnp.float32
    tiles = PLANE // LANES

    def stay(x):
        return pltpu.with_memory_space_constraint(x, pltpu.HBM)

    def view6(x):
        return stay(x.reshape(6, depth, tiles, LANES))

    def view1(x):
        return stay(x.reshape(depth, tiles, LANES))

    pick_shape = (groups, 7, BLK // LANES, LANES)
    plane = (NVX, LANES)
    flat = (tiles, LANES)
    dma = pltpu.SemaphoreType.DMA
    ints = [pltpu.SMEM(x.shape, jnp.int32) for x in (substeps, pull_group, pull_block, owner)]
    six, one = pltpu.VMEM((6, depth) + flat, f32), pltpu.VMEM((depth,) + flat, f32)
    field = jax.ShapeDtypeStruct((3, depth + 4) + plane, f32)
    *fields, weights, inbox, element_sums = pl.pallas_call(
        functools.partial(rve_kernel, depth, groups, slabs, in_dev, volume),
        in_specs=[hbm] * 11,
        out_specs=[vmem] * 8,
        out_shape=[
            *[field] * ITERS,
            jax.ShapeDtypeStruct((ITERS, 8, LANES), f32),
            jax.ShapeDtypeStruct((7, BLK // LANES, in_dev, LANES), f32),
            jax.ShapeDtypeStruct((1, 42), f32),
        ],
        scratch_shapes=[
            *ints,
            six, one, six, six, one, one, one,
            pltpu.VMEM((7, depth) + plane, f32),
            pltpu.VMEM((8 + len(PAIRS), 8, LANES), f32),
            pltpu.VMEM((7, depth) + flat, f32),
            pltpu.VMEM((7,) + flat, f32),
            pltpu.VMEM(pick_shape, f32),
            pltpu.VMEM((2, 3) + plane, f32),
            pltpu.VMEM((depth + 4,) + plane, f32),
            pltpu.VMEM((depth + 4,) + plane, f32),
            pltpu.VMEM((16, LANES), f32),
            pltpu.VMEM((slabs, 16, LANES), f32),
            pltpu.VMEM((8, LANES), f32),
            pltpu.VMEM((slabs, 8, LANES), f32),
            pltpu.VMEM(pick_shape, f32),
            pltpu.VMEM((groups, 8, LANES), f32),
            pltpu.VMEM((8, LANES), f32),
            pltpu.VMEM((8, LANES), f32),
            pltpu.VMEM((slabs, 8, LANES), f32),
            pltpu.VMEM((2 * LANES, LANES), jnp.bfloat16),
            pltpu.VMEM((2 * LANES, LANES), jnp.bfloat16),
            pltpu.VMEM((2, 5) + flat, f32),
            pltpu.VMEM((2, 5) + flat, f32),
            pltpu.VMEM(((ITERS + 1) // 2, 3, 2, 2) + flat, f32),
            pltpu.VMEM(((ITERS + 1) // 2, 3, 2, 2) + flat, f32),
            dma((max(depth, 5), 7)),
            dma((4,)),
            dma((ITERS + 1, 3, 2)),
            dma((ITERS + 1, 3, 2)),
            dma((3, slabs)),
            dma((3, slabs)),
            dma((groups,)),
            dma((groups,)),
            dma((groups,)),
            dma((groups,)),
        ],
        compiler_params=pltpu.CompilerParams(
            collective_id=0, has_side_effects=True, vmem_limit_bytes=32 * 1024 * 1024
        ),
        name="rve_step",
    )(
        stay(substeps), stay(pull_group), stay(pull_block), stay(owner),
        view6(plastic_strain), view1(hardening_var), view6(strain_start), view6(strain_step),
        view1(shear_mod), view1(bulk_mod), view1(yield_stress),
    )
    correction, inbox, element_sums = pl.pallas_call(
        functools.partial(result_kernel, depth),
        in_specs=[vmem] * 8,
        out_specs=[hbm] * 3,
        out_shape=[
            jax.ShapeDtypeStruct((3, depth, tiles, LANES), f32),
            jax.ShapeDtypeStruct((7, BLK // LANES, in_dev, LANES), f32),
            jax.ShapeDtypeStruct((1, 42), f32),
        ],
        scratch_shapes=[pltpu.VMEM((3, depth) + flat, f32), dma((depth,)), dma((2,))],
        compiler_params=pltpu.CompilerParams(vmem_limit_bytes=8 * 1024 * 1024),
        name="result",
    )(*fields, weights, inbox, element_sums)
    correction = correction.reshape(3, 1, depth, PLANE)
    inbox = inbox.swapaxes(1, 2).reshape(7, 1, in_dev, BLK)
    return correction, inbox, element_sums


def solution(mesh):
    return jax.shard_map(
        functools.partial(on_device, mesh.shape["rve"], mesh.shape["slab"]),
        mesh=mesh,
        in_specs=(
            P(None, "rve", "slab", None),
            P("rve", "slab", None),
            P(None, "rve", "slab", None),
            P(None, "rve", "slab", None),
            P("rve", "slab", None),
            P("rve", "slab", None),
            P("rve", "slab", None),
            P(),
            P(),
            P(),
            P(),
        ),
        out_specs=(P(None, "rve", "slab", None), P(None, "rve", "slab", None), P("rve", None)),
        check_vma=False,
    )
```

```python
import functools
import math

import jax
import jax.numpy as jnp
from jax import lax
from jax.experimental import pallas as pl
from jax.experimental.pallas import tpu as pltpu
from jax.sharding import PartitionSpec as P

NVX = 96
ITERS = 5
SUBMAX = 8
PLANE = 9216
BLK = 2304
LANES = 128
PART = 24
MEAN_LANE = 42
SHIFT = 12.0
MESH = pl.DeviceIdType.MESH

hard_ratio = 0.3
mass_weight = 0.05
root_two_thirds = math.sqrt(2.0 / 3.0)
half_root = 1.0 / math.sqrt(2.0)
KEPT = (0, 1, 3, 4, 5)
PAIRS = tuple((i, j) for i in range(5) for j in range(i, 5))


def lane_id(rows):
    return lax.broadcasted_iota(jnp.int32, (rows, LANES), 1)


def unpack_rows(a, b, c):
    lane = lane_id(a.shape[0])
    plain = (
        a,
        pltpu.roll(jnp.where(lane >= 96, a, b), 32, 1),
        pltpu.roll(jnp.where(lane >= 64, b, c), 64, 1),
        pltpu.roll(c, 96, 1),
    )
    return plain


def pack_rows(rows4):
    t0, t1, t2, t3 = rows4
    lane = lane_id(t0.shape[0])
    r1, r2, r3 = pltpu.roll(t1, 96, 1), pltpu.roll(t2, 64, 1), pltpu.roll(t3, 32, 1)
    return (
        jnp.where(lane < 96, t0, r1),
        jnp.where(lane < 64, r1, r2),
        jnp.where(lane < 32, r2, r3),
    )


def norm_form(a, b):
    return (
        a[0] * (b[0] + b[0] + b[1]) + a[1] * (b[0] + b[1] + b[1])
        + a[2] * b[2] + a[3] * b[3] + a[4] * b[4]
    )


def deviator(vals):
    trace = vals[0] + vals[1] + vals[2]
    third = trace * (1.0 / 3.0)
    return [vals[0] - third, vals[1] - third, vals[3], vals[4], vals[5]], trace


def full(five):
    return [five[0], five[1], -(five[0] + five[1]), five[2], five[3], five[4]]


def material_plane(z, counts, ins, st_ref, acc_ref, hist_ref, tmp_ref):
    p_ref, h_ref, b_ref, d_ref, g_ref, k_ref, y_ref = ins
    tiles = PLANE // LANES
    parts = tuple(slice(t, t + PART) for t in range(0, tiles, PART))
    quarter_rows = BLK // LANES

    def strains(rows):
        dev0, tr0 = deviator([b_ref[c, z, rows] - p_ref[c, z, rows] for c in range(6)])
        devs, trs = deviator([d_ref[c, z, rows] for c in range(6)])
        return dev0, devs, tr0 + trs

    state = []
    for rows in parts:
        row = lax.broadcasted_iota(jnp.int32, (PART, LANES), 0) + rows.start
        count = jnp.full((PART, LANES), counts[0], jnp.int32)
        for q in range(1, 4):
            count = jnp.where(row >= q * quarter_rows, counts[q], count)
        count = count.astype(jnp.float32)
        inv = 1.0 / count
        dev0, devs, _ = strains(rows)
        s00 = norm_form(dev0, dev0)
        s01 = 2.0 * inv * norm_form(dev0, devs)
        s11 = inv * inv * norm_form(devs, devs)
        level = (11.0 * root_two_thirds / 2.2) * (
            y_ref[z, rows] / g_ref[z, rows] + hard_ratio * h_ref[z, rows]
        )
        state.append([jnp.ones_like(inv), count - float(SUBMAX), level, level, s00, s01, s11, inv])
    for turn in range(SUBMAX - 1):
        for one in state:
            a, b, level, _, s00, s01, s11, _ = one
            b = b + 1.0
            square = jnp.maximum(a * (a * s00 + b * s01) + (b * b) * s11, 1e-30)
            rs = lax.rsqrt(square)
            fac = jnp.minimum((1.0 + level * rs) * (1.0 / 11.0), 1.0)
            fac = jnp.where(b > 0.0, fac, 1.0)
            one[2] = level + (1.0 - fac) * (square * rs)
            one[0] = a * fac
            one[1] = b * fac
    sums = [None] * (8 + len(PAIRS))
    for rows, one in zip(parts, state):
        a, b, level, level0, _, _, _, inv = one
        b = (b + 1.0) * inv
        dev0, devs, trace = strains(rows)
        dd = [a * x + b * y for x, y in zip(dev0, devs)]
        square = jnp.maximum(norm_form(dd, dd), 1e-30)
        rs = lax.rsqrt(square)
        fac = jnp.minimum((1.0 + level * rs) * (1.0 / 11.0), 1.0)
        level = level + (1.0 - fac) * (square * rs)
        fin = [fac * v for v in dd]
        mu = g_ref[z, rows]
        coef = mu * fac
        weight = (coef - mu) * (rs * rs)
        bulk = k_ref[z, rows]
        vol = bulk * trace
        two_mu = 2.0 * mu
        ms = [two_mu * v for v in fin]
        wn = [weight * v for v in dd]
        gone = full([x + y - w for x, y, w in zip(dev0, devs, fin)])
        for c, v in enumerate(full(ms)):
            tmp_ref[c, rows] = v + vol if c < 3 else v
            hist_ref[c, z, rows] = p_ref[c, z, rows] + gone[c]
        tmp_ref[6, rows] = coef
        hist_ref[6, z, rows] = h_ref[z, rows] + root_two_thirds * (level - level0)
        terms = [vol, bulk, coef] + ms + [wn[i] * dd[j] for i, j in PAIRS]
        for t, v in enumerate(terms):
            for o in range(0, PART, 8):
                piece = v[o : o + 8]
                sums[t] = piece if sums[t] is None else sums[t] + piece
    for t, v in enumerate(sums):
        acc_ref[t] += v
    for f in range(7):
        for g in range(tiles // 24):
            a, b, c = (tmp_ref[f, pl.ds(3 * g + k, 8, stride=9)] for k in range(3))
            for r, rowv in enumerate(unpack_rows(a, b, c)):
                at = 8 * (4 * g + r)
                st_ref[f, z, at : at + 8] = rowv


def summary_row(acc_ref, volume):
    tot = [
        jnp.sum(acc_ref[t], axis=(0, 1), keepdims=True) * (1.0 / volume)
        for t in range(8 + len(PAIRS))
    ]
    vol, bulk, coef = tot[0], tot[1], tot[2]
    ms = tot[3:8]
    stress = [vol + ms[0], vol + ms[1], vol - ms[0] - ms[1], ms[2], ms[3], ms[4]]
    table = {}
    for t, (i, j) in enumerate(PAIRS):
        table[(KEPT[i], KEPT[j])] = tot[8 + t]
        table[(KEPT[j], KEPT[i])] = tot[8 + t]
    for j in KEPT:
        table[(2, j)] = -(table[(0, j)] + table[(1, j)])
        table[(j, 2)] = table[(2, j)]
    table[(2, 2)] = -(table[(2, 0)] + table[(2, 1)])
    lane = lane_id(1)
    row = jnp.zeros((1, LANES), jnp.float32)
    for c in range(6):
        row = jnp.where(lane == c, stress[c], row)
    for i in range(6):
        for j in range(6):
            v = 2.0 * table[(i, j)]
            if i == j:
                v = v + 2.0 * coef
            if i < 3 and j < 3:
                v = v + bulk - (2.0 / 3.0) * coef
            row = jnp.where(lane == 6 + 6 * i + j, v, row)
    return jnp.where(lane == MEAN_LANE, coef, row)


def ring_next(pieces):
    return pieces[1:] + [pltpu.roll(pieces[0], 7, 0)]


def ring_prev(pieces):
    return [pltpu.roll(pieces[-1], 1, 0)] + pieces[:-1]


def cut(v):
    return [v[i : i + 8] for i in range(0, v.shape[0], 8)]


def fold(pieces):
    lane = lane_id(8)
    return [
        jnp.where(lane < NVX, pieces[i], pltpu.roll(pieces[9 + i // 3], 96 - 32 * (i % 3), 1))
        for i in range(9)
    ]


def unfold(pieces):
    lane = lane_id(8)
    out = list(pieces)
    for m in range(3):
        a, b, c = (pltpu.roll(pieces[3 * m + k], 32 + 32 * k, 1) for k in range(3))
        out.append(jnp.where(lane < 32, a, jnp.where(lane < 64, b, c)))
    return out


def column_matrix(centre, after, before):
    row = lax.broadcasted_iota(jnp.int32, (2 * LANES, LANES), 0)
    lane = lax.broadcasted_iota(jnp.int32, (2 * LANES, LANES), 1)
    row = jnp.where(row >= LANES, row - LANES, row)
    gap = row - lane
    weight = jnp.where(
        gap == 0, centre,
        jnp.where(
            (gap == 1) | (gap == 1 - NVX), after,
            jnp.where((gap == -1) | (gap == NVX - 1), before, 0.0),
        ),
    )
    return jnp.where((row < NVX) & (lane < NVX), weight, 0.0).astype(jnp.bfloat16)


def spread_rows(pieces):
    p = [x + y for x, y in zip(pieces, ring_next(pieces))]
    return [x + y for x, y in zip(p, ring_prev(p))]


def split(v):
    high = v.astype(jnp.bfloat16)
    low = (v - high.astype(jnp.float32)).astype(jnp.bfloat16)
    return jnp.concatenate([high, low], axis=1)


def columns(v, matrix):
    return jnp.dot(split(v), matrix, preferred_element_type=jnp.float32)


def tree(values):
    while len(values) > 1:
        pairs = [x + y for x, y in zip(values[::2], values[1::2])]
        values = pairs + values[2 * len(pairs) :]
    return values[0]


def inner(a, b):
    total = a[0] * b[0]
    for x, y in zip(a[1:], b[1:]):
        total = total + x * y
    return total


def combine(moments, shift):
    one = jnp.ones_like(moments[0])
    res_c, dir_c, out = [one], [one], []
    res_m, dir_m = list(moments), list(moments)
    norm = moments[0]
    for turn in range(ITERS):
        image_m = [shift * x + y for x, y in zip(dir_m, dir_m[1:])]
        alpha = norm / inner(dir_c, image_m)
        grown = out + [jnp.zeros_like(one)]
        out = [x + alpha * y for x, y in zip(grown, dir_c)]
        if turn == ITERS - 1:
            return out
        image_c = [shift * dir_c[0]]
        image_c += [shift * x + y for x, y in zip(dir_c[1:], dir_c)] + [dir_c[-1]]
        res_c = [x - alpha * y for x, y in zip(res_c, image_c)] + [-alpha * image_c[-1]]
        res_m = [x - alpha * y for x, y in zip(res_m, image_m)]
        norm_next = inner(res_c, res_m)
        beta = norm_next / norm
        norm = norm_next
        dir_c = [x + beta * y for x, y in zip(res_c, dir_c)] + [res_c[-1]]
        dir_m = [x + beta * y for x, y in zip(res_m, dir_m)]


def rve_kernel(
    depth, groups, slabs, in_dev, volume,
    sub_in, pg_in, pb_in, own_in, p_in, h_in, b_in, d_in, g_in, k_in, y_in,
    v0, v1, v2, v3, v4, w_ref, inbox_ref, elem_ref,
    sub_ref, pg_ref, pb_ref, own_ref,
    p_ref, h_ref, b_ref, d_ref, g_ref, k_ref, y_ref,
    st_ref, acc_ref, hist_ref, tmp_ref, pick_ref,
    sh, c8, ee, ps, red, ms, mr, ab, es, eo, th, tr, tt, td, sp, sr, pk, rk,
    insem, smallsem,
    nsend, nrecv, rsend, rrecv, bsend, brecv, esend, erecv,
):
    group = lax.axis_index("rve")
    slab = lax.axis_index("slab")
    up = lax.rem(slab + 1, slabs)
    down = lax.rem(slab + slabs - 1, slabs)
    last = depth - 1
    vv = (v0, v1, v2, v3, v4)
    ins = (p_ref, h_ref, b_ref, d_ref, g_ref, k_ref, y_ref)
    sources = (p_in, h_in, b_in, d_in, g_in, k_in, y_in)

    early = max(min(6, depth), 2 * (depth // 3))

    chunks = [(0, 0, 1), (0, last, 1), (2, 1, early // 2 - 1), (2, depth - early // 2, early // 2 - 1)]
    chunks.append((early, early // 2, depth - early))
    if depth % 2:
        chunks = [(i, i // 2 if i % 2 == 0 else last - i // 2, 1) for i in range(depth)]
    chunks = [chunk for chunk in chunks if chunk[2] > 0]

    def fetch(n, k):
        at = pl.ds(chunks[n][1], chunks[n][2])
        wide = len(ins[k].shape) == 4
        return pltpu.make_async_copy(
            sources[k].at[:, at] if wide else sources[k].at[at],
            ins[k].at[:, at] if wide else ins[k].at[at],
            insem.at[n, k],
        )

    small = [
        pltpu.make_async_copy(src, dst, smallsem.at[i])
        for i, (src, dst) in enumerate(
            ((sub_in, sub_ref), (pg_in, pg_ref), (pb_in, pb_ref), (own_in, own_ref))
        )
    ]
    small[0].start()
    for n in range(len(chunks)):
        for k in range(7):
            fetch(n, k).start()
    for copy in small[1:]:
        copy.start()
    barrier = pltpu.get_barrier_semaphore()
    for k in range(1, slabs):
        pl.semaphore_signal(
            barrier, inc=1, device_id={"slab": lax.rem(slab + k, slabs)}, device_id_type=MESH
        )
    for k in range(1, groups):
        pl.semaphore_signal(
            barrier, inc=1, device_id={"rve": lax.rem(group + k, groups)}, device_id_type=MESH
        )

    def remote(src, dst, ssem, rsem, axis, to):
        return pltpu.make_async_remote_copy(
            src_ref=src, dst_ref=dst, send_sem=ssem, recv_sem=rsem,
            device_id={axis: to}, device_id_type=MESH,
        )

    def to_slabs(src, dst, ssem, rsem):
        copies = []
        for k in range(1, slabs):
            to = lax.rem(slab + k, slabs)
            copies.append(remote(src, dst.at[slab], ssem.at[k], rsem.at[k], "slab", to))
        return copies

    acc_ref[...] = jnp.zeros_like(acc_ref)
    tt[...] = column_matrix(2.0, 1.0, 1.0)
    td[...] = column_matrix(0.0, 1.0, -1.0)
    small[0].wait()

    def stress_copies(part):
        at = (slice(0, 3), slice(3, 5))[part]
        return [
            remote(
                sp.at[side, at], sr.at[side, at],
                nsend.at[0, part, side], nrecv.at[0, part, side], "slab", to,
            )
            for side, to in enumerate((up, down))
        ]

    def pack_plane(v, into, at):
        for i, piece in enumerate(fold(cut(v))):
            into[(*at, slice(8 * i, 8 * i + 8))] = piece

    def pack_stress():
        for side, z in enumerate((last, 0)):
            for n, f in enumerate((2, 3, 4)):
                pack_plane(st_ref[f, z], sp, (side, n))

    def pack_coefficient():
        for side, zs in enumerate(((last - 1, last), (0, 1))):
            for n, z in enumerate(zs):
                pack_plane(st_ref[6, z], sp, (side, 3 + n))

    def unpack_stress():
        for side in range(2):
            for n in range(3):
                for i, v in enumerate(unfold(cut(sr[side, n]))):
                    sh[side, n, 8 * i : 8 * i + 8] = v

    def unpack_coefficient():
        for side, zs in enumerate(((0, 1), (depth + 2, depth + 3))):
            for n, z in enumerate(zs):
                for i, v in enumerate(unfold(cut(sr[side, 3 + n]))):
                    c8[z, 8 * i : 8 * i + 8] = 0.125 * v

    def ydiff(v):
        v = cut(v)
        both = [x - y for x, y in zip(ring_next(v), ring_prev(v))]
        return jnp.concatenate(both, axis=0)

    def rhs_plane(z, below, above):
        s3, s4, s5 = st_ref[3, z], st_ref[4, z], st_ref[5, z]
        zd = {c: above(c) - below(c) for c in (2, 3, 4)}
        hr = 0.5 * half_root
        xd = columns(jnp.concatenate([st_ref[0, z], s5, s4], axis=0), td[...])
        f0 = 0.5 * xd[0:NVX] + hr * (ydiff(s5) + zd[4])
        f1 = hr * (xd[NVX : 2 * NVX] + zd[3]) + 0.5 * ydiff(st_ref[1, z])
        f2 = hr * (xd[2 * NVX :] + ydiff(s3)) + 0.5 * zd[2]
        for c, v in enumerate((f0, f1, f2)):
            v0[c, z + 2] = v

    def field_copies(j, c):
        if j + 1 == ITERS:
            pairs = [(pk.at[j // 2, c, 0, 1], rk.at[j // 2, c, 0, 1], up)]
        else:
            pairs = [(pk.at[j // 2, c, n], rk.at[j // 2, c, n], to) for n, to in ((0, up), (1, down))]
        return [
            remote(src, dst, nsend.at[1 + j, c, side], nrecv.at[1 + j, c, side], "slab", to)
            for side, (src, dst, to) in enumerate(pairs)
        ]

    def pack_edges(j, c):
        if j + 1 == ITERS:
            pack_plane(vv[j][c, depth + 1], pk, (j // 2, c, 0, 1))
            return
        for side, zs in enumerate(((depth, depth + 1), (2, 3))):
            for n, z in enumerate(zs):
                pack_plane(vv[j][c, z], pk, (j // 2, c, side, n))

    def unpack_halos(j, c):
        if j + 1 == ITERS:
            for i, v in enumerate(unfold(cut(rk[j // 2, c, 0, 1]))):
                vv[j][c, 1, 8 * i : 8 * i + 8] = v + v
            return
        for side, zs in enumerate(((0, 1), (depth + 2, depth + 3))):
            for n, z in enumerate(zs):
                for i, v in enumerate(unfold(cut(rk[j // 2, c, side, n]))):
                    vv[j][c, z, 8 * i : 8 * i + 8] = v

    def start(copies):
        for copy in copies:
            copy.start()

    def finish(copies):
        for copy in copies:
            copy.wait()

    def material(i):
        z = i // 2 + (i % 2) * (last - 2 * (i // 2))
        base = (slab * depth + z) * 4
        counts = [sub_ref[group, base + q] for q in range(4)]
        material_plane(z, counts, ins, st_ref, acc_ref, hist_ref, tmp_ref)
        c8[z + 2] = st_ref[6, z] * 0.125

    def material_step(turn, _):
        for first in sorted({chunk[0] for chunk in chunks}):

            @pl.when(turn == first)
            def _():
                for n, chunk in enumerate(chunks):
                    if chunk[0] == first:
                        finish([fetch(n, k) for k in range(7)])

        material(turn)

        @pl.when(turn == 1)
        def _():
            pl.semaphore_wait(barrier, slabs + groups - 2)
            pack_stress()
            start(stress_copies(0))

        @pl.when(turn == min(3, last))
        def _():
            pack_coefficient()
            start(stress_copies(1))

        @pl.when(turn == early - 1)
        def _():
            th[...] = acc_ref[2]
            start(to_slabs(th, tr, rsend.at[2], rrecv.at[2]))
            finish(stress_copies(0))
            unpack_stress()
            for z in sorted({0, 1, last - 1, last}):
                rhs_plane(
                    z,
                    lambda c, z=z: st_ref[c, z - 1] if z > 0 else sh[0, c - 2],
                    lambda c, z=z: st_ref[c, z + 1] if z < last else sh[1, c - 2],
                )
            for c in range(3):
                pack_edges(0, c)
                start(field_copies(0, c))

        return 0

    lax.fori_loop(0, depth, material_step, 0)
    def rhs_inner(z, _):
        rhs_plane(z, lambda c: st_ref[c, z - 1], lambda c: st_ref[c, z + 1])
        return 0

    if last - 1 > 2:
        lax.fori_loop(2, last - 1, rhs_inner, 0, unroll=min(4, last - 3))
    finish(stress_copies(1))
    unpack_coefficient()
    tr[slab] = th[...]
    finish(to_slabs(th, tr, rsend.at[2], rrecv.at[2]))
    total = tr[0]
    for k in range(1, slabs):
        total = total + tr[k]
    shift = (SHIFT / (early * slabs * PLANE)) * jnp.sum(total, axis=(0, 1), keepdims=True)

    def diagonal(z, _):
        wide = spread_rows(cut(c8[z - 1] + 2.0 * c8[z] + c8[z + 1]))
        wide = cut(columns(jnp.concatenate(wide, axis=0), tt[...]))
        for i, w in enumerate(wide):
            at = slice(8 * i, 8 * i + 8)
            ee[z, at] = (8.0 * (8.0 + mass_weight) * c8[z, at] - shift) + w
        return 0

    lax.fori_loop(1, depth + 3, diagonal, 0, unroll=min(7, depth + 2))

    zero = jnp.zeros((8, LANES), jnp.float32)

    def apply_plane(j, c, z, carry):
        norm, curve = carry
        plain, mixed, norms, curves = [], [], [], []
        for i in range(0, NVX, 8):
            at = slice(i, i + 8)
            ra, rb, rc = vv[j][c, z - 1, at], vv[j][c, z, at], vv[j][c, z + 1, at]
            crb = c8[z, at] * rb
            plain.append((ra + rc) + (rb + rb))
            mixed.append((c8[z - 1, at] * ra + c8[z + 1, at] * rc) + (crb + crb))
        both = jnp.concatenate(spread_rows(plain) + spread_rows(mixed), axis=0)
        both = columns(both, tt[...])
        plain, mixed = cut(both[0:NVX]), cut(both[NVX:])
        for i in range(0, NVX, 8):
            at = slice(i, i + 8)
            rb = vv[j][c, z, at]
            image = ee[z, at] * rb - c8[z, at] * plain[i // 8] - mixed[i // 8]
            if j + 1 < ITERS:
                vv[j + 1][c, z, at] = image
            norms.append(rb * rb)
            curves.append(rb * image)
        if z < 2 or z > depth + 1:
            return carry
        return norm + tree(norms), curve + tree(curves)

    own = range(2, depth + 2)
    outer = list(dict.fromkeys((2, depth + 1, 3, depth)))

    def apply_planes(j, c, zs, carry):
        for z in zs:
            carry = apply_plane(j, c, z, carry)
        return carry

    for c in range(3):
        vv[ITERS - 1][c, depth + 2] = jnp.zeros((NVX, LANES), jnp.float32)
    for j in range(ITERS):

        first = outer if j + 2 < ITERS else (depth + 1, depth)

        def with_send(c, carry):
            carry = apply_planes(j, c, first, carry)
            pack_edges(j + 1, c)
            start(field_copies(j + 1, c))
            return carry

        def others(c, carry):
            return apply_planes(j, c, [z for z in own if z not in first], carry)

        def inside(c, carry):
            return apply_planes(j, c, range(3, depth + 1 if j + 1 < ITERS else depth + 2), carry)

        def outside(c, carry):
            finish(field_copies(j, c))
            unpack_halos(j, c)
            return apply_planes(j, c, (1, 2, depth + 1, depth + 2), carry)

        carry = (zero, zero)
        if j % 2:
            carry = lax.fori_loop(0, 3, with_send, carry)
            carry = lax.fori_loop(0, 3, others, carry)
        else:
            carry = lax.fori_loop(0, 3, inside, carry)
            if j == 2:
                eo[...] = jnp.broadcast_to(summary_row(acc_ref, volume), (8, LANES))
                means = to_slabs(eo, mr, rsend.at[0], rrecv.at[0])
                start(means)
                mr[slab] = eo[...]
                for copy in small[1:]:
                    copy.wait()
                quarter_rows = BLK // LANES
                for g in range(groups):
                    chosen = slab * (4 * depth)
                    for n in range(in_dev):
                        slot = slab * in_dev + n
                        chosen = jnp.where(pg_ref[g, slot] == group, pb_ref[g, slot], chosen)
                    chosen = jnp.clip(chosen - slab * (4 * depth), 0, 4 * depth - 1)
                    z = chosen // 4
                    quarter = chosen - 4 * z
                    for c in range(7):
                        plane = hist_ref[c, z]
                        got = plane[0:quarter_rows]
                        for q in range(1, 4):
                            got = jnp.where(quarter == q, plane[q * quarter_rows : (q + 1) * quarter_rows], got)
                        pick_ref[g, c] = got
                moves = []
                for k in range(1, groups):
                    to = lax.rem(group + k, groups)
                    move = remote(pick_ref.at[to], ab.at[group], bsend.at[k], brecv.at[k], "rve", to)
                    move.start()
                    moves.append(move)
                ab[group] = pick_ref[group]
            if j + 1 < ITERS:
                carry = lax.fori_loop(0, 3, outside, carry)
            else:
                for c in range(3):
                    finish(field_copies(j, c))
                for c in range(3):
                    unpack_halos(j, c)
                for c in range(3):
                    carry = apply_plane(j, c, 2, carry)
        if j == 3:
            finish(means)
            total = mr[0]
            for k in range(1, slabs):
                total = total + mr[k]
            ms[...] = total
            element = [
                remote(ms, es.at[group], esend.at[k], erecv.at[k], "rve", lax.rem(group + k, groups))
                for k in range(1, groups)
            ]
            start(element)
            es[group] = total
        ps[2 * j : 2 * j + 1] = jnp.sum(carry[0], axis=0, keepdims=True)
        ps[2 * j + 1 : 2 * j + 2] = jnp.sum(carry[1], axis=0, keepdims=True)
    ps[2 * ITERS :] = jnp.zeros((ps.shape[0] - 2 * ITERS, LANES), jnp.float32)

    copies = to_slabs(ps, red, rsend.at[1], rrecv.at[1])
    start(copies)
    red[slab] = ps[...]
    for move in moves:
        move.wait()
    for j in range(in_dev):
        source = pg_ref[group, slab * in_dev + j]
        got = ab[jnp.clip(source, 0, groups - 1)]
        for c in range(7):
            inbox_ref[c, :, j, :] = got[c]
    for copy in element:
        copy.wait()
    mine = jnp.zeros((1, LANES), jnp.float32)
    for k in range(groups):
        mine = mine + jnp.where(own_ref[k] == group, es[k][0:1], 0.0)
    elem_ref[...] = mine[:, 0:42]

    for copy in copies:
        copy.wait()
    moments = red[0]
    for k in range(1, slabs):
        moments = moments + red[k]
    moments = jnp.where(lane_id(ps.shape[0]) < NVX, moments, 0.0)
    moments = jnp.sum(moments, axis=1, keepdims=True)
    weights = combine([moments[k : k + 1] for k in range(2 * ITERS)], shift)
    for j, w in enumerate(weights):
        w_ref[j] = jnp.broadcast_to(w, (8, LANES))


def result_kernel(
    depth, v0, v1, v2, v3, v4, w_ref, inbox_ref, elem_ref,
    out_hbm, inbox_hbm, elem_hbm, out_ref, sems, othersems,
):
    others = [
        pltpu.make_async_copy(inbox_ref, inbox_hbm, othersems.at[0]),
        pltpu.make_async_copy(elem_ref, elem_hbm, othersems.at[1]),
    ]
    for copy in others:
        copy.start()
    weights = [w_ref[j] for j in range(ITERS)]

    def leave(z):
        return pltpu.make_async_copy(out_ref.at[:, z], out_hbm.at[:, z], sems.at[z])

    def to_flat(z, _):
        for c in range(3):
            for g in range(NVX // 32):
                rows4 = []
                for r in range(4):
                    at = slice(8 * (4 * g + r), 8 * (4 * g + r) + 8)
                    rows4.append(inner(weights, [v[c, z + 2, at] for v in (v0, v1, v2, v3, v4)]))
                for t, v in enumerate(pack_rows(rows4)):
                    out_ref[c, z, pl.ds(3 * g + t, 8, stride=9)] = v
        leave(z).start()
        return 0

    lax.fori_loop(0, depth, to_flat, 0, unroll=min(4, depth))

    def left(z, _):
        leave(z).wait()
        return 0

    lax.fori_loop(0, depth, left, 0)
    for copy in others:
        copy.wait()


def on_device(
    groups, slabs,
    plastic_strain, hardening_var, strain_start, strain_step, shear_mod, bulk_mod, yield_stress,
    substeps, pull_group, pull_block, owner,
):
    depth = plastic_strain.shape[2]
    in_dev = pull_group.shape[1] // slabs
    volume = float(depth * slabs * PLANE)
    vmem = pl.BlockSpec(memory_space=pltpu.VMEM)
    hbm = pl.BlockSpec(memory_space=pl.ANY)
    f32 = jnp.float32
    tiles = PLANE // LANES

    def stay(x):
        return pltpu.with_memory_space_constraint(x, pltpu.HBM)

    def view6(x):
        return stay(x.reshape(6, depth, tiles, LANES))

    def view1(x):
        return stay(x.reshape(depth, tiles, LANES))

    pick_shape = (groups, 7, BLK // LANES, LANES)
    plane = (NVX, LANES)
    flat = (tiles, LANES)
    dma = pltpu.SemaphoreType.DMA
    ints = [pltpu.SMEM(x.shape, jnp.int32) for x in (substeps, pull_group, pull_block, owner)]
    six, one = pltpu.VMEM((6, depth) + flat, f32), pltpu.VMEM((depth,) + flat, f32)
    field = jax.ShapeDtypeStruct((3, depth + 4) + plane, f32)
    *fields, weights, inbox, element_sums = pl.pallas_call(
        functools.partial(rve_kernel, depth, groups, slabs, in_dev, volume),
        in_specs=[hbm] * 11,
        out_specs=[vmem] * 8,
        out_shape=[
            *[field] * ITERS,
            jax.ShapeDtypeStruct((ITERS, 8, LANES), f32),
            jax.ShapeDtypeStruct((7, BLK // LANES, in_dev, LANES), f32),
            jax.ShapeDtypeStruct((1, 42), f32),
        ],
        scratch_shapes=[
            *ints,
            six, one, six, six, one, one, one,
            pltpu.VMEM((7, depth) + plane, f32),
            pltpu.VMEM((8 + len(PAIRS), 8, LANES), f32),
            pltpu.VMEM((7, depth) + flat, f32),
            pltpu.VMEM((7,) + flat, f32),
            pltpu.VMEM(pick_shape, f32),
            pltpu.VMEM((2, 3) + plane, f32),
            pltpu.VMEM((depth + 4,) + plane, f32),
            pltpu.VMEM((depth + 4,) + plane, f32),
            pltpu.VMEM((16, LANES), f32),
            pltpu.VMEM((slabs, 16, LANES), f32),
            pltpu.VMEM((8, LANES), f32),
            pltpu.VMEM((slabs, 8, LANES), f32),
            pltpu.VMEM(pick_shape, f32),
            pltpu.VMEM((groups, 8, LANES), f32),
            pltpu.VMEM((8, LANES), f32),
            pltpu.VMEM((8, LANES), f32),
            pltpu.VMEM((slabs, 8, LANES), f32),
            pltpu.VMEM((2 * LANES, LANES), jnp.bfloat16),
            pltpu.VMEM((2 * LANES, LANES), jnp.bfloat16),
            pltpu.VMEM((2, 5) + flat, f32),
            pltpu.VMEM((2, 5) + flat, f32),
            pltpu.VMEM(((ITERS + 1) // 2, 3, 2, 2) + flat, f32),
            pltpu.VMEM(((ITERS + 1) // 2, 3, 2, 2) + flat, f32),
            dma((max(depth, 5), 7)),
            dma((4,)),
            dma((ITERS + 1, 3, 2)),
            dma((ITERS + 1, 3, 2)),
            dma((3, slabs)),
            dma((3, slabs)),
            dma((groups,)),
            dma((groups,)),
            dma((groups,)),
            dma((groups,)),
        ],
        compiler_params=pltpu.CompilerParams(
            collective_id=0, has_side_effects=True, vmem_limit_bytes=32 * 1024 * 1024
        ),
        name="rve_step",
    )(
        stay(substeps), stay(pull_group), stay(pull_block), stay(owner),
        view6(plastic_strain), view1(hardening_var), view6(strain_start), view6(strain_step),
        view1(shear_mod), view1(bulk_mod), view1(yield_stress),
    )
    correction, inbox, element_sums = pl.pallas_call(
        functools.partial(result_kernel, depth),
        in_specs=[vmem] * 8,
        out_specs=[hbm] * 3,
        out_shape=[
            jax.ShapeDtypeStruct((3, depth, tiles, LANES), f32),
            jax.ShapeDtypeStruct((7, BLK // LANES, in_dev, LANES), f32),
            jax.ShapeDtypeStruct((1, 42), f32),
        ],
        scratch_shapes=[pltpu.VMEM((3, depth) + flat, f32), dma((depth,)), dma((2,))],
        compiler_params=pltpu.CompilerParams(vmem_limit_bytes=8 * 1024 * 1024),
        name="result",
    )(*fields, weights, inbox, element_sums)
    correction = correction.reshape(3, 1, depth, PLANE)
    inbox = inbox.swapaxes(1, 2).reshape(7, 1, in_dev, BLK)
    return correction, inbox, element_sums


def solution(mesh):
    return jax.shard_map(
        functools.partial(on_device, mesh.shape["rve"], mesh.shape["slab"]),
        mesh=mesh,
        in_specs=(
            P(None, "rve", "slab", None),
            P("rve", "slab", None),
            P(None, "rve", "slab", None),
            P(None, "rve", "slab", None),
            P("rve", "slab", None),
            P("rve", "slab", None),
            P("rve", "slab", None),
            P(),
            P(),
            P(),
            P(),
        ),
        out_specs=(P(None, "rve", "slab", None), P(None, "rve", "slab", None), P("rve", None)),
        check_vma=False,
    )
```

```python
import functools
import math

import jax
import jax.numpy as jnp
from jax import lax
from jax.experimental import pallas as pl
from jax.experimental.pallas import tpu as pltpu
from jax.sharding import PartitionSpec as P

NVX = 96
ITERS = 5
SUBMAX = 8
PLANE = 9216
BLK = 2304
LANES = 128
PART = 72
MEAN_LANE = 42
SHIFT = 12.0
MESH = pl.DeviceIdType.MESH

hard_ratio = 0.3
mass_weight = 0.05
root_two_thirds = math.sqrt(2.0 / 3.0)
half_root = 1.0 / math.sqrt(2.0)
KEPT = (0, 1, 3, 4, 5)
PAIRS = tuple((i, j) for i in range(5) for j in range(i, 5))


def lane_id(rows):
    return lax.broadcasted_iota(jnp.int32, (rows, LANES), 1)


def unpack_rows(a, b, c):
    lane = lane_id(a.shape[0])
    plain = (
        a,
        pltpu.roll(jnp.where(lane >= 96, a, b), 32, 1),
        pltpu.roll(jnp.where(lane >= 64, b, c), 64, 1),
        pltpu.roll(c, 96, 1),
    )
    return plain


def pack_rows(rows4):
    t0, t1, t2, t3 = rows4
    lane = lane_id(t0.shape[0])
    r1, r2, r3 = pltpu.roll(t1, 96, 1), pltpu.roll(t2, 64, 1), pltpu.roll(t3, 32, 1)
    return (
        jnp.where(lane < 96, t0, r1),
        jnp.where(lane < 64, r1, r2),
        jnp.where(lane < 32, r2, r3),
    )


def norm_form(a, b):
    return (
        a[0] * (b[0] + b[0] + b[1]) + a[1] * (b[0] + b[1] + b[1])
        + a[2] * b[2] + a[3] * b[3] + a[4] * b[4]
    )


def deviator(vals):
    trace = vals[0] + vals[1] + vals[2]
    third = trace * (1.0 / 3.0)
    return [vals[0] - third, vals[1] - third, vals[3], vals[4], vals[5]], trace


def full(five):
    return [five[0], five[1], -(five[0] + five[1]), five[2], five[3], five[4]]


def material_plane(z, counts, ins, st_ref, acc_ref, hist_ref, tmp_ref):
    p_ref, h_ref, b_ref, d_ref, g_ref, k_ref, y_ref = ins
    tiles = PLANE // LANES
    parts = tuple(slice(t, t + PART) for t in range(0, tiles, PART))
    quarter_rows = BLK // LANES

    def strains(rows):
        dev0, tr0 = deviator([b_ref[c, z, rows] - p_ref[c, z, rows] for c in range(6)])
        devs, trs = deviator([d_ref[c, z, rows] for c in range(6)])
        return dev0, devs, tr0 + trs

    state = []
    for rows in parts:
        row = lax.broadcasted_iota(jnp.int32, (PART, LANES), 0) + rows.start
        count = jnp.full((PART, LANES), counts[0], jnp.int32)
        for q in range(1, 4):
            count = jnp.where(row >= q * quarter_rows, counts[q], count)
        count = count.astype(jnp.float32)
        inv = 1.0 / count
        dev0, devs, _ = strains(rows)
        s00 = norm_form(dev0, dev0)
        s01 = 2.0 * inv * norm_form(dev0, devs)
        s11 = inv * inv * norm_form(devs, devs)
        level = (11.0 * root_two_thirds / 2.2) * (
            y_ref[z, rows] / g_ref[z, rows] + hard_ratio * h_ref[z, rows]
        )
        state.append([jnp.ones_like(inv), count - float(SUBMAX), level, level, s00, s01, s11, inv])
    for turn in range(SUBMAX - 1):
        for one in state:
            a, b, level, _, s00, s01, s11, _ = one
            b = b + 1.0
            square = jnp.maximum(a * (a * s00 + b * s01) + (b * b) * s11, 1e-30)
            rs = lax.rsqrt(square)
            fac = jnp.minimum((1.0 + level * rs) * (1.0 / 11.0), 1.0)
            fac = jnp.where(b > 0.0, fac, 1.0)
            one[2] = level + (1.0 - fac) * (square * rs)
            one[0] = a * fac
            one[1] = b * fac
    sums = [None] * (8 + len(PAIRS))
    for rows, one in zip(parts, state):
        a, b, level, level0, _, _, _, inv = one
        b = (b + 1.0) * inv
        dev0, devs, trace = strains(rows)
        dd = [a * x + b * y for x, y in zip(dev0, devs)]
        square = jnp.maximum(norm_form(dd, dd), 1e-30)
        rs = lax.rsqrt(square)
        fac = jnp.minimum((1.0 + level * rs) * (1.0 / 11.0), 1.0)
        level = level + (1.0 - fac) * (square * rs)
        fin = [fac * v for v in dd]
        mu = g_ref[z, rows]
        coef = mu * fac
        weight = (coef - mu) * (rs * rs)
        bulk = k_ref[z, rows]
        vol = bulk * trace
        two_mu = 2.0 * mu
        ms = [two_mu * v for v in fin]
        wn = [weight * v for v in dd]
        gone = full([x + y - w for x, y, w in zip(dev0, devs, fin)])
        for c, v in enumerate(full(ms)):
            tmp_ref[c, rows] = v + vol if c < 3 else v
            hist_ref[c, z, rows] = p_ref[c, z, rows] + gone[c]
        tmp_ref[6, rows] = coef
        hist_ref[6, z, rows] = h_ref[z, rows] + root_two_thirds * (level - level0)
        terms = [vol, bulk, coef] + ms + [wn[i] * dd[j] for i, j in PAIRS]
        for t, v in enumerate(terms):
            for o in range(0, PART, 8):
                piece = v[o : o + 8]
                sums[t] = piece if sums[t] is None else sums[t] + piece
    for t, v in enumerate(sums):
        acc_ref[t] += v
    for f in range(7):
        for g in range(tiles // 24):
            a, b, c = (tmp_ref[f, pl.ds(3 * g + k, 8, stride=9)] for k in range(3))
            for r, rowv in enumerate(unpack_rows(a, b, c)):
                at = 8 * (4 * g + r)
                st_ref[f, z, at : at + 8] = rowv


def summary_row(acc_ref, volume):
    tot = [
        jnp.sum(acc_ref[t], axis=(0, 1), keepdims=True) * (1.0 / volume)
        for t in range(8 + len(PAIRS))
    ]
    vol, bulk, coef = tot[0], tot[1], tot[2]
    ms = tot[3:8]
    stress = [vol + ms[0], vol + ms[1], vol - ms[0] - ms[1], ms[2], ms[3], ms[4]]
    table = {}
    for t, (i, j) in enumerate(PAIRS):
        table[(KEPT[i], KEPT[j])] = tot[8 + t]
        table[(KEPT[j], KEPT[i])] = tot[8 + t]
    for j in KEPT:
        table[(2, j)] = -(table[(0, j)] + table[(1, j)])
        table[(j, 2)] = table[(2, j)]
    table[(2, 2)] = -(table[(2, 0)] + table[(2, 1)])
    lane = lane_id(1)
    row = jnp.zeros((1, LANES), jnp.float32)
    for c in range(6):
        row = jnp.where(lane == c, stress[c], row)
    for i in range(6):
        for j in range(6):
            v = 2.0 * table[(i, j)]
            if i == j:
                v = v + 2.0 * coef
            if i < 3 and j < 3:
                v = v + bulk - (2.0 / 3.0) * coef
            row = jnp.where(lane == 6 + 6 * i + j, v, row)
    return jnp.where(lane == MEAN_LANE, coef, row)


def ring_next(pieces):
    return pieces[1:] + [pltpu.roll(pieces[0], 7, 0)]


def ring_prev(pieces):
    return [pltpu.roll(pieces[-1], 1, 0)] + pieces[:-1]


def cut(v):
    return [v[i : i + 8] for i in range(0, v.shape[0], 8)]


def fold(pieces):
    lane = lane_id(8)
    return [
        jnp.where(lane < NVX, pieces[i], pltpu.roll(pieces[9 + i // 3], 96 - 32 * (i % 3), 1))
        for i in range(9)
    ]


def unfold(pieces):
    lane = lane_id(8)
    out = list(pieces)
    for m in range(3):
        a, b, c = (pltpu.roll(pieces[3 * m + k], 32 + 32 * k, 1) for k in range(3))
        out.append(jnp.where(lane < 32, a, jnp.where(lane < 64, b, c)))
    return out


def column_matrix(centre, after, before):
    row = lax.broadcasted_iota(jnp.int32, (2 * LANES, LANES), 0)
    lane = lax.broadcasted_iota(jnp.int32, (2 * LANES, LANES), 1)
    row = jnp.where(row >= LANES, row - LANES, row)
    gap = row - lane
    weight = jnp.where(
        gap == 0, centre,
        jnp.where(
            (gap == 1) | (gap == 1 - NVX), after,
            jnp.where((gap == -1) | (gap == NVX - 1), before, 0.0),
        ),
    )
    return jnp.where((row < NVX) & (lane < NVX), weight, 0.0).astype(jnp.bfloat16)


def spread_rows(pieces):
    p = [x + y for x, y in zip(pieces, ring_next(pieces))]
    return [x + y for x, y in zip(p, ring_prev(p))]


def split(v):
    high = v.astype(jnp.bfloat16)
    low = (v - high.astype(jnp.float32)).astype(jnp.bfloat16)
    return jnp.concatenate([high, low], axis=1)


def columns(v, matrix):
    return jnp.dot(split(v), matrix, preferred_element_type=jnp.float32)


def tree(values):
    while len(values) > 1:
        pairs = [x + y for x, y in zip(values[::2], values[1::2])]
        values = pairs + values[2 * len(pairs) :]
    return values[0]


def inner(a, b):
    total = a[0] * b[0]
    for x, y in zip(a[1:], b[1:]):
        total = total + x * y
    return total


def combine(moments, shift):
    one = jnp.ones_like(moments[0])
    res_c, dir_c, out = [one], [one], []
    res_m, dir_m = list(moments), list(moments)
    norm = moments[0]
    for turn in range(ITERS):
        image_m = [shift * x + y for x, y in zip(dir_m, dir_m[1:])]
        alpha = norm / inner(dir_c, image_m)
        grown = out + [jnp.zeros_like(one)]
        out = [x + alpha * y for x, y in zip(grown, dir_c)]
        if turn == ITERS - 1:
            return out
        image_c = [shift * dir_c[0]]
        image_c += [shift * x + y for x, y in zip(dir_c[1:], dir_c)] + [dir_c[-1]]
        res_c = [x - alpha * y for x, y in zip(res_c, image_c)] + [-alpha * image_c[-1]]
        res_m = [x - alpha * y for x, y in zip(res_m, image_m)]
        norm_next = inner(res_c, res_m)
        beta = norm_next / norm
        norm = norm_next
        dir_c = [x + beta * y for x, y in zip(res_c, dir_c)] + [res_c[-1]]
        dir_m = [x + beta * y for x, y in zip(res_m, dir_m)]


def rve_kernel(
    depth, groups, slabs, in_dev, volume,
    sub_in, pg_in, pb_in, own_in, p_in, h_in, b_in, d_in, g_in, k_in, y_in,
    v0, v1, v2, v3, v4, w_ref, inbox_ref, elem_ref,
    sub_ref, pg_ref, pb_ref, own_ref,
    p_ref, h_ref, b_ref, d_ref, g_ref, k_ref, y_ref,
    st_ref, acc_ref, hist_ref, tmp_ref, pick_ref,
    sh, c8, ee, ps, red, ms, mr, ab, es, eo, th, tr, tt, td, sp, sr, pk, rk,
    insem, smallsem,
    nsend, nrecv, rsend, rrecv, bsend, brecv, esend, erecv,
):
    group = lax.axis_index("rve")
    slab = lax.axis_index("slab")
    up = lax.rem(slab + 1, slabs)
    down = lax.rem(slab + slabs - 1, slabs)
    last = depth - 1
    vv = (v0, v1, v2, v3, v4)
    ins = (p_ref, h_ref, b_ref, d_ref, g_ref, k_ref, y_ref)
    sources = (p_in, h_in, b_in, d_in, g_in, k_in, y_in)

    early = max(min(6, depth), 2 * (depth // 3))

    chunks = [(0, 0, 1), (0, last, 1), (2, 1, early // 2 - 1), (2, depth - early // 2, early // 2 - 1)]
    chunks.append((early, early // 2, depth - early))
    if depth % 2:
        chunks = [(i, i // 2 if i % 2 == 0 else last - i // 2, 1) for i in range(depth)]
    chunks = [chunk for chunk in chunks if chunk[2] > 0]

    def fetch(n, k):
        at = pl.ds(chunks[n][1], chunks[n][2])
        wide = len(ins[k].shape) == 4
        return pltpu.make_async_copy(
            sources[k].at[:, at] if wide else sources[k].at[at],
            ins[k].at[:, at] if wide else ins[k].at[at],
            insem.at[n, k],
        )

    small = [
        pltpu.make_async_copy(src, dst, smallsem.at[i])
        for i, (src, dst) in enumerate(
            ((sub_in, sub_ref), (pg_in, pg_ref), (pb_in, pb_ref), (own_in, own_ref))
        )
    ]
    small[0].start()
    for n in range(len(chunks)):
        for k in range(7):
            fetch(n, k).start()
    for copy in small[1:]:
        copy.start()
    barrier = pltpu.get_barrier_semaphore()
    for k in range(1, slabs):
        pl.semaphore_signal(
            barrier, inc=1, device_id={"slab": lax.rem(slab + k, slabs)}, device_id_type=MESH
        )
    for k in range(1, groups):
        pl.semaphore_signal(
            barrier, inc=1, device_id={"rve": lax.rem(group + k, groups)}, device_id_type=MESH
        )

    def remote(src, dst, ssem, rsem, axis, to):
        return pltpu.make_async_remote_copy(
            src_ref=src, dst_ref=dst, send_sem=ssem, recv_sem=rsem,
            device_id={axis: to}, device_id_type=MESH,
        )

    def to_slabs(src, dst, ssem, rsem):
        copies = []
        for k in range(1, slabs):
            to = lax.rem(slab + k, slabs)
            copies.append(remote(src, dst.at[slab], ssem.at[k], rsem.at[k], "slab", to))
        return copies

    acc_ref[...] = jnp.zeros_like(acc_ref)
    tt[...] = column_matrix(2.0, 1.0, 1.0)
    td[...] = column_matrix(0.0, 1.0, -1.0)
    small[0].wait()

    def stress_copies(part):
        at = (slice(0, 3), slice(3, 5))[part]
        return [
            remote(
                sp.at[side, at], sr.at[side, at],
                nsend.at[0, part, side], nrecv.at[0, part, side], "slab", to,
            )
            for side, to in enumerate((up, down))
        ]

    def pack_plane(v, into, at):
        for i, piece in enumerate(fold(cut(v))):
            into[(*at, slice(8 * i, 8 * i + 8))] = piece

    def pack_stress():
        for side, z in enumerate((last, 0)):
            for n, f in enumerate((2, 3, 4)):
                pack_plane(st_ref[f, z], sp, (side, n))

    def pack_coefficient():
        for side, zs in enumerate(((last - 1, last), (0, 1))):
            for n, z in enumerate(zs):
                pack_plane(st_ref[6, z], sp, (side, 3 + n))

    def unpack_stress():
        for side in range(2):
            for n in range(3):
                for i, v in enumerate(unfold(cut(sr[side, n]))):
                    sh[side, n, 8 * i : 8 * i + 8] = v

    def unpack_coefficient():
        for side, zs in enumerate(((0, 1), (depth + 2, depth + 3))):
            for n, z in enumerate(zs):
                for i, v in enumerate(unfold(cut(sr[side, 3 + n]))):
                    c8[z, 8 * i : 8 * i + 8] = 0.125 * v

    def ydiff(v):
        v = cut(v)
        both = [x - y for x, y in zip(ring_next(v), ring_prev(v))]
        return jnp.concatenate(both, axis=0)

    def rhs_plane(z, below, above):
        s3, s4, s5 = st_ref[3, z], st_ref[4, z], st_ref[5, z]
        zd = {c: above(c) - below(c) for c in (2, 3, 4)}
        hr = 0.5 * half_root
        xd = columns(jnp.concatenate([st_ref[0, z], s5, s4], axis=0), td[...])
        f0 = 0.5 * xd[0:NVX] + hr * (ydiff(s5) + zd[4])
        f1 = hr * (xd[NVX : 2 * NVX] + zd[3]) + 0.5 * ydiff(st_ref[1, z])
        f2 = hr * (xd[2 * NVX :] + ydiff(s3)) + 0.5 * zd[2]
        for c, v in enumerate((f0, f1, f2)):
            v0[c, z + 2] = v

    def field_copies(j, c):
        if j + 1 == ITERS:
            pairs = [(pk.at[j // 2, c, 0, 1], rk.at[j // 2, c, 0, 1], up)]
        else:
            pairs = [(pk.at[j // 2, c, n], rk.at[j // 2, c, n], to) for n, to in ((0, up), (1, down))]
        return [
            remote(src, dst, nsend.at[1 + j, c, side], nrecv.at[1 + j, c, side], "slab", to)
            for side, (src, dst, to) in enumerate(pairs)
        ]

    def pack_edges(j, c):
        if j + 1 == ITERS:
            pack_plane(vv[j][c, depth + 1], pk, (j // 2, c, 0, 1))
            return
        for side, zs in enumerate(((depth, depth + 1), (2, 3))):
            for n, z in enumerate(zs):
                pack_plane(vv[j][c, z], pk, (j // 2, c, side, n))

    def unpack_halos(j, c):
        if j + 1 == ITERS:
            for i, v in enumerate(unfold(cut(rk[j // 2, c, 0, 1]))):
                vv[j][c, 1, 8 * i : 8 * i + 8] = v + v
            return
        for side, zs in enumerate(((0, 1), (depth + 2, depth + 3))):
            for n, z in enumerate(zs):
                for i, v in enumerate(unfold(cut(rk[j // 2, c, side, n]))):
                    vv[j][c, z, 8 * i : 8 * i + 8] = v

    def start(copies):
        for copy in copies:
            copy.start()

    def finish(copies):
        for copy in copies:
            copy.wait()

    def material(i):
        z = i // 2 + (i % 2) * (last - 2 * (i // 2))
        base = (slab * depth + z) * 4
        counts = [sub_ref[group, base + q] for q in range(4)]
        material_plane(z, counts, ins, st_ref, acc_ref, hist_ref, tmp_ref)
        c8[z + 2] = st_ref[6, z] * 0.125

    def material_step(turn, _):
        for first in sorted({chunk[0] for chunk in chunks}):

            @pl.when(turn == first)
            def _():
                for n, chunk in enumerate(chunks):
                    if chunk[0] == first:
                        finish([fetch(n, k) for k in range(7)])

        material(turn)

        @pl.when(turn == 1)
        def _():
            pl.semaphore_wait(barrier, slabs + groups - 2)
            pack_stress()
            start(stress_copies(0))

        @pl.when(turn == min(3, last))
        def _():
            pack_coefficient()
            start(stress_copies(1))

        @pl.when(turn == early - 1)
        def _():
            th[...] = acc_ref[2]
            start(to_slabs(th, tr, rsend.at[2], rrecv.at[2]))
            finish(stress_copies(0))
            unpack_stress()
            for z in sorted({0, 1, last - 1, last}):
                rhs_plane(
                    z,
                    lambda c, z=z: st_ref[c, z - 1] if z > 0 else sh[0, c - 2],
                    lambda c, z=z: st_ref[c, z + 1] if z < last else sh[1, c - 2],
                )
            for c in range(3):
                pack_edges(0, c)
                start(field_copies(0, c))

        return 0

    lax.fori_loop(0, depth, material_step, 0)
    def rhs_inner(z, _):
        rhs_plane(z, lambda c: st_ref[c, z - 1], lambda c: st_ref[c, z + 1])
        return 0

    if last - 1 > 2:
        lax.fori_loop(2, last - 1, rhs_inner, 0, unroll=min(4, last - 3))
    finish(stress_copies(1))
    unpack_coefficient()
    tr[slab] = th[...]
    finish(to_slabs(th, tr, rsend.at[2], rrecv.at[2]))
    total = tr[0]
    for k in range(1, slabs):
        total = total + tr[k]
    shift = (SHIFT / (early * slabs * PLANE)) * jnp.sum(total, axis=(0, 1), keepdims=True)

    def diagonal(z, _):
        wide = spread_rows(cut(c8[z - 1] + 2.0 * c8[z] + c8[z + 1]))
        wide = cut(columns(jnp.concatenate(wide, axis=0), tt[...]))
        for i, w in enumerate(wide):
            at = slice(8 * i, 8 * i + 8)
            ee[z, at] = (8.0 * (8.0 + mass_weight) * c8[z, at] - shift) + w
        return 0

    lax.fori_loop(1, depth + 3, diagonal, 0, unroll=min(7, depth + 2))

    zero = jnp.zeros((8, LANES), jnp.float32)

    def apply_plane(j, c, z, carry):
        norm, curve = carry
        plain, mixed, norms, curves = [], [], [], []
        for i in range(0, NVX, 8):
            at = slice(i, i + 8)
            ra, rb, rc = vv[j][c, z - 1, at], vv[j][c, z, at], vv[j][c, z + 1, at]
            crb = c8[z, at] * rb
            plain.append((ra + rc) + (rb + rb))
            mixed.append((c8[z - 1, at] * ra + c8[z + 1, at] * rc) + (crb + crb))
        both = jnp.concatenate(spread_rows(plain) + spread_rows(mixed), axis=0)
        both = columns(both, tt[...])
        plain, mixed = cut(both[0:NVX]), cut(both[NVX:])
        for i in range(0, NVX, 8):
            at = slice(i, i + 8)
            rb = vv[j][c, z, at]
            image = ee[z, at] * rb - c8[z, at] * plain[i // 8] - mixed[i // 8]
            if j + 1 < ITERS:
                vv[j + 1][c, z, at] = image
            norms.append(rb * rb)
            curves.append(rb * image)
        if z < 2 or z > depth + 1:
            return carry
        return norm + tree(norms), curve + tree(curves)

    own = range(2, depth + 2)
    outer = list(dict.fromkeys((2, depth + 1, 3, depth)))

    def apply_planes(j, c, zs, carry):
        for z in zs:
            carry = apply_plane(j, c, z, carry)
        return carry

    for c in range(3):
        vv[ITERS - 1][c, depth + 2] = jnp.zeros((NVX, LANES), jnp.float32)
    for j in range(ITERS):

        first = outer if j + 2 < ITERS else (depth + 1, depth)

        def with_send(c, carry):
            carry = apply_planes(j, c, first, carry)
            pack_edges(j + 1, c)
            start(field_copies(j + 1, c))
            return carry

        def others(c, carry):
            return apply_planes(j, c, [z for z in own if z not in first], carry)

        def inside(c, carry):
            return apply_planes(j, c, range(3, depth + 1 if j + 1 < ITERS else depth + 2), carry)

        def outside(c, carry):
            finish(field_copies(j, c))
            unpack_halos(j, c)
            return apply_planes(j, c, (1, 2, depth + 1, depth + 2), carry)

        carry = (zero, zero)
        if j % 2:
            carry = lax.fori_loop(0, 3, with_send, carry)
            carry = lax.fori_loop(0, 3, others, carry)
        else:
            carry = lax.fori_loop(0, 3, inside, carry)
            if j == 2:
                eo[...] = jnp.broadcast_to(summary_row(acc_ref, volume), (8, LANES))
                means = to_slabs(eo, mr, rsend.at[0], rrecv.at[0])
                start(means)
                mr[slab] = eo[...]
                for copy in small[1:]:
                    copy.wait()
                quarter_rows = BLK // LANES
                for g in range(groups):
                    chosen = slab * (4 * depth)
                    for n in range(in_dev):
                        slot = slab * in_dev + n
                        chosen = jnp.where(pg_ref[g, slot] == group, pb_ref[g, slot], chosen)
                    chosen = jnp.clip(chosen - slab * (4 * depth), 0, 4 * depth - 1)
                    z = chosen // 4
                    quarter = chosen - 4 * z
                    for c in range(7):
                        plane = hist_ref[c, z]
                        got = plane[0:quarter_rows]
                        for q in range(1, 4):
                            got = jnp.where(quarter == q, plane[q * quarter_rows : (q + 1) * quarter_rows], got)
                        pick_ref[g, c] = got
                moves = []
                for k in range(1, groups):
                    to = lax.rem(group + k, groups)
                    move = remote(pick_ref.at[to], ab.at[group], bsend.at[k], brecv.at[k], "rve", to)
                    move.start()
                    moves.append(move)
                ab[group] = pick_ref[group]
            if j + 1 < ITERS:
                carry = lax.fori_loop(0, 3, outside, carry)
            else:
                for c in range(3):
                    finish(field_copies(j, c))
                for c in range(3):
                    unpack_halos(j, c)
                for c in range(3):
                    carry = apply_plane(j, c, 2, carry)
        if j == 3:
            finish(means)
            total = mr[0]
            for k in range(1, slabs):
                total = total + mr[k]
            ms[...] = total
            element = [
                remote(ms, es.at[group], esend.at[k], erecv.at[k], "rve", lax.rem(group + k, groups))
                for k in range(1, groups)
            ]
            start(element)
            es[group] = total
        ps[2 * j : 2 * j + 1] = jnp.sum(carry[0], axis=0, keepdims=True)
        ps[2 * j + 1 : 2 * j + 2] = jnp.sum(carry[1], axis=0, keepdims=True)
    ps[2 * ITERS :] = jnp.zeros((ps.shape[0] - 2 * ITERS, LANES), jnp.float32)

    copies = to_slabs(ps, red, rsend.at[1], rrecv.at[1])
    start(copies)
    red[slab] = ps[...]
    for move in moves:
        move.wait()
    for j in range(in_dev):
        source = pg_ref[group, slab * in_dev + j]
        got = ab[jnp.clip(source, 0, groups - 1)]
        for c in range(7):
            inbox_ref[c, :, j, :] = got[c]
    for copy in element:
        copy.wait()
    mine = jnp.zeros((1, LANES), jnp.float32)
    for k in range(groups):
        mine = mine + jnp.where(own_ref[k] == group, es[k][0:1], 0.0)
    elem_ref[...] = mine[:, 0:42]

    for copy in copies:
        copy.wait()
    moments = red[0]
    for k in range(1, slabs):
        moments = moments + red[k]
    moments = jnp.where(lane_id(ps.shape[0]) < NVX, moments, 0.0)
    moments = jnp.sum(moments, axis=1, keepdims=True)
    weights = combine([moments[k : k + 1] for k in range(2 * ITERS)], shift)
    for j, w in enumerate(weights):
        w_ref[j] = jnp.broadcast_to(w, (8, LANES))


def result_kernel(
    depth, v0, v1, v2, v3, v4, w_ref, inbox_ref, elem_ref,
    out_hbm, inbox_hbm, elem_hbm, out_ref, sems, othersems,
):
    others = [
        pltpu.make_async_copy(inbox_ref, inbox_hbm, othersems.at[0]),
        pltpu.make_async_copy(elem_ref, elem_hbm, othersems.at[1]),
    ]
    for copy in others:
        copy.start()
    weights = [w_ref[j] for j in range(ITERS)]

    def leave(z):
        return pltpu.make_async_copy(out_ref.at[:, z], out_hbm.at[:, z], sems.at[z])

    def to_flat(z, _):
        for c in range(3):
            for g in range(NVX // 32):
                rows4 = []
                for r in range(4):
                    at = slice(8 * (4 * g + r), 8 * (4 * g + r) + 8)
                    rows4.append(inner(weights, [v[c, z + 2, at] for v in (v0, v1, v2, v3, v4)]))
                for t, v in enumerate(pack_rows(rows4)):
                    out_ref[c, z, pl.ds(3 * g + t, 8, stride=9)] = v
        leave(z).start()
        return 0

    lax.fori_loop(0, depth, to_flat, 0, unroll=min(4, depth))

    def left(z, _):
        leave(z).wait()
        return 0

    lax.fori_loop(0, depth, left, 0)
    for copy in others:
        copy.wait()


def on_device(
    groups, slabs,
    plastic_strain, hardening_var, strain_start, strain_step, shear_mod, bulk_mod, yield_stress,
    substeps, pull_group, pull_block, owner,
):
    depth = plastic_strain.shape[2]
    in_dev = pull_group.shape[1] // slabs
    volume = float(depth * slabs * PLANE)
    vmem = pl.BlockSpec(memory_space=pltpu.VMEM)
    hbm = pl.BlockSpec(memory_space=pl.ANY)
    f32 = jnp.float32
    tiles = PLANE // LANES

    def stay(x):
        return pltpu.with_memory_space_constraint(x, pltpu.HBM)

    def view6(x):
        return stay(x.reshape(6, depth, tiles, LANES))

    def view1(x):
        return stay(x.reshape(depth, tiles, LANES))

    pick_shape = (groups, 7, BLK // LANES, LANES)
    plane = (NVX, LANES)
    flat = (tiles, LANES)
    dma = pltpu.SemaphoreType.DMA
    ints = [pltpu.SMEM(x.shape, jnp.int32) for x in (substeps, pull_group, pull_block, owner)]
    six, one = pltpu.VMEM((6, depth) + flat, f32), pltpu.VMEM((depth,) + flat, f32)
    field = jax.ShapeDtypeStruct((3, depth + 4) + plane, f32)
    *fields, weights, inbox, element_sums = pl.pallas_call(
        functools.partial(rve_kernel, depth, groups, slabs, in_dev, volume),
        in_specs=[hbm] * 11,
        out_specs=[vmem] * 8,
        out_shape=[
            *[field] * ITERS,
            jax.ShapeDtypeStruct((ITERS, 8, LANES), f32),
            jax.ShapeDtypeStruct((7, BLK // LANES, in_dev, LANES), f32),
            jax.ShapeDtypeStruct((1, 42), f32),
        ],
        scratch_shapes=[
            *ints,
            six, one, six, six, one, one, one,
            pltpu.VMEM((7, depth) + plane, f32),
            pltpu.VMEM((8 + len(PAIRS), 8, LANES), f32),
            pltpu.VMEM((7, depth) + flat, f32),
            pltpu.VMEM((7,) + flat, f32),
            pltpu.VMEM(pick_shape, f32),
            pltpu.VMEM((2, 3) + plane, f32),
            pltpu.VMEM((depth + 4,) + plane, f32),
            pltpu.VMEM((depth + 4,) + plane, f32),
            pltpu.VMEM((16, LANES), f32),
            pltpu.VMEM((slabs, 16, LANES), f32),
            pltpu.VMEM((8, LANES), f32),
            pltpu.VMEM((slabs, 8, LANES), f32),
            pltpu.VMEM(pick_shape, f32),
            pltpu.VMEM((groups, 8, LANES), f32),
            pltpu.VMEM((8, LANES), f32),
            pltpu.VMEM((8, LANES), f32),
            pltpu.VMEM((slabs, 8, LANES), f32),
            pltpu.VMEM((2 * LANES, LANES), jnp.bfloat16),
            pltpu.VMEM((2 * LANES, LANES), jnp.bfloat16),
            pltpu.VMEM((2, 5) + flat, f32),
            pltpu.VMEM((2, 5) + flat, f32),
            pltpu.VMEM(((ITERS + 1) // 2, 3, 2, 2) + flat, f32),
            pltpu.VMEM(((ITERS + 1) // 2, 3, 2, 2) + flat, f32),
            dma((max(depth, 5), 7)),
            dma((4,)),
            dma((ITERS + 1, 3, 2)),
            dma((ITERS + 1, 3, 2)),
            dma((3, slabs)),
            dma((3, slabs)),
            dma((groups,)),
            dma((groups,)),
            dma((groups,)),
            dma((groups,)),
        ],
        compiler_params=pltpu.CompilerParams(
            collective_id=0, has_side_effects=True, vmem_limit_bytes=32 * 1024 * 1024
        ),
        name="rve_step",
    )(
        stay(substeps), stay(pull_group), stay(pull_block), stay(owner),
        view6(plastic_strain), view1(hardening_var), view6(strain_start), view6(strain_step),
        view1(shear_mod), view1(bulk_mod), view1(yield_stress),
    )
    correction, inbox, element_sums = pl.pallas_call(
        functools.partial(result_kernel, depth),
        in_specs=[vmem] * 8,
        out_specs=[hbm] * 3,
        out_shape=[
            jax.ShapeDtypeStruct((3, depth, tiles, LANES), f32),
            jax.ShapeDtypeStruct((7, BLK // LANES, in_dev, LANES), f32),
            jax.ShapeDtypeStruct((1, 42), f32),
        ],
        scratch_shapes=[pltpu.VMEM((3, depth) + flat, f32), dma((depth,)), dma((2,))],
        compiler_params=pltpu.CompilerParams(vmem_limit_bytes=8 * 1024 * 1024),
        name="result",
    )(*fields, weights, inbox, element_sums)
    correction = correction.reshape(3, 1, depth, PLANE)
    inbox = inbox.swapaxes(1, 2).reshape(7, 1, in_dev, BLK)
    return correction, inbox, element_sums


def solution(mesh):
    return jax.shard_map(
        functools.partial(on_device, mesh.shape["rve"], mesh.shape["slab"]),
        mesh=mesh,
        in_specs=(
            P(None, "rve", "slab", None),
            P("rve", "slab", None),
            P(None, "rve", "slab", None),
            P(None, "rve", "slab", None),
            P("rve", "slab", None),
            P("rve", "slab", None),
            P("rve", "slab", None),
            P(),
            P(),
            P(),
            P(),
        ),
        out_specs=(P(None, "rve", "slab", None), P(None, "rve", "slab", None), P("rve", None)),
        check_vma=False,
    )
```
